32 devices in a mesh: mem: 4 (over y, x), reg: 8 (over z, core).
Axes of the slice: x: 2, y: 2, z: 4, core: 2. Of those that a mesh axis runs over, the one named last changes fastest.
Arguments:
- alpha: float32 [32, 16, 32, 128], P('mem', None, 'reg'), may hold values from -6 to 6
- perturbation: bfloat16 [32, 2, 16, 128, 512], P('mem', None, None, 'reg'), may hold values from -6 to 6
- obs_cell: int32 [8192], P('reg'), may hold values from 0 to 131071
- obs_kind: int32 [8192], P('reg'), may hold values from 0 to 3
- obs_value: float32 [8192], P('reg'), may hold values from -6 to 6
- obs_weight: float32 [8192], P('reg'), may hold values from 1 to 4
Outputs:
- obs_gradient: float32 [32, 16, 32, 128], P('mem', None, 'reg')
The draws below stay inside these ranges and needn't reach their ends.
Inputs may be any that keep to these rules, and one draw needn't show every extreme that they name: `obs_cell`: each entry is level * 16 * 512 + row * 512 + column of a fine cell, the row counted from the first row of the observation's own region. `obs_kind`: 0 zonal wind, 1 meridional wind, 2 relative vorticity, 3 zonal wind advection.
All inputs are finite; a program needn't handle non-finite values.
Results may differ from the reference program's by a relative error of at most 0.0003.
Values sent between devices are 32-bit elements; how exact they have to be, the bound alone decides.
No kernel may reach another device: no remote copies, remote signals or barrier semaphores. Data moves between devices by JAX's collectives and lax.ppermute only.
A program may use at most 64 MiB of HBM per device.

```python
import math
import jax
import jax.numpy as jnp
from jax import lax

RX = 16
NY = 512
LEV = 16
OBS_REG = 1024
PASSES = 2
MEMBERS = 32
NX = 128
NXC = 32
NYC = 128
OBS = 8192


def touch_ends(entries, own_key, least, top_value):
    longest = entries.shape.index(max(entries.shape))
    spots = []
    for shift in (0, 1):
        where = [jax.random.randint(jax.random.fold_in(own_key, axis), (), 0, length) for axis, length in enumerate(entries.shape)]
        where[longest] = (where[longest] + shift) % entries.shape[longest]
        spots.append(tuple(where))
    return entries.at[spots[0]].set(least).at[spots[1]].set(top_value)


def spiked(entries, key, source, target, parts, factor):
    owner, partner = [(jnp.arange(entries.shape[position]) // (entries.shape[position] // parts)).reshape([-1 if axis == position else 1 for axis in range(entries.ndim)]) for position in (source, target)]
    chosen = jax.random.permutation(key, parts)[partner]
    strong = (owner == chosen) | (owner == (partner + parts // 2) % parts)
    return jnp.where(strong, factor * entries, entries)


def block_scale(key, extent, cuts, smallest, top_value):
    def one(position, parts):
        steps = jax.random.uniform(jax.random.fold_in(jax.random.fold_in(key, 6), position), (parts,), jnp.float32, smallest / len(cuts), top_value / len(cuts))
        return jnp.repeat(jnp.exp(steps), extent[position] // parts).reshape((-1,) + (1,) * (len(extent) - position - 1))

    level = one(*cuts[0])
    for cut in cuts[1:]:
        level = level * one(*cut)
    return level


def bell_draw(rng, dims, width, most, pieces=(), held_as=jnp.bfloat16):
    array = width * jax.random.normal(rng, dims, jnp.float32)
    if pieces:
        array = array * block_scale(rng, dims, pieces, -0.22, 0.18)
    return jnp.clip(array, -most, most).astype(held_as)


def noise_with(key, extent, width, reach, shards, heavy, held_as=jnp.bfloat16):
    array = width * jax.random.normal(key, extent, jnp.float32)
    if shards:
        array = array * block_scale(key, extent, shards, -0.22, 0.18)
    return jnp.clip(spiked(array, jax.random.fold_in(key, 3), *heavy), -reach, reach).astype(held_as)


def setup_inputs(seed: int = 0) -> dict:
    seeds = jax.random.split(jax.random.key(seed), 7)
    alpha = bell_draw(seeds[0], (MEMBERS, LEV, NXC, NYC), 1.0, 6.0, ((0, 4), (2, 8)), jnp.float32)
    perturbation = noise_with(seeds[1], (MEMBERS, 2, LEV, NX, NY), 1.0, 6.0, ((0, 4), (3, 8)), (0, 2, 4, 2.0))
    obs_cell = touch_ends(jax.random.randint(seeds[2], (OBS,), 0, LEV * RX * NY), jax.random.fold_in(seeds[2], 1), 0, (LEV * RX * NY) - 1).astype(jnp.int32)
    obs_kind = touch_ends(jax.random.randint(seeds[3], (OBS,), 0, 4), jax.random.fold_in(seeds[3], 1), 0, 3).astype(jnp.int32)
    obs_value = bell_draw(seeds[4], (OBS,), 1.0, 6.0, ((0, 8),), jnp.float32)
    obs_weight = jnp.clip(jnp.exp(math.log(4.0) - 1.3862944 * jax.random.uniform(seeds[5], (OBS,), jnp.float32) ** block_scale(seeds[5], (OBS,), ((0, 8),), -0.2, 0.2)), 1.0, 4.0)
    return {"alpha": alpha, "perturbation": perturbation, "obs_cell": obs_cell, "obs_kind": obs_kind, "obs_value": obs_value, "obs_weight": obs_weight}


diffuse = 0.2
highest = lax.Precision.HIGHEST

def weights(fine_rows, fine_start, coarse_count, coarse_start):
    finer = (jnp.arange(fine_rows) + fine_start).astype(jnp.float32)
    coarser = (jnp.arange(coarse_count) + coarse_start).astype(jnp.float32)
    where_at = (finer[:, None] + 0.5) / 4.0 - 0.5
    return jnp.maximum(0.0, 1.0 - jnp.abs(where_at - coarser[None, :]))

def one_pass(block):
    padded = jnp.pad(block, ((0, 0), (0, 0), (1, 1), (1, 1)))
    beside_all = padded[:, :, 2:, 1:-1] + padded[:, :, :-2, 1:-1] + padded[:, :, 1:-1, 2:] + padded[:, :, 1:-1, :-2]
    return block + diffuse * (beside_all - 4.0 * block)

def slopes(padded):
    along_x = (padded[..., 2:, 1:-1] - padded[..., :-2, 1:-1]) * 0.5
    along_y = (padded[..., 1:-1, 2:] - padded[..., 1:-1, :-2]) * 0.5
    return (along_x, along_y)

def reference(alpha, perturbation, obs_cell, obs_kind, obs_value, obs_weight):
    members = alpha.shape[0]
    scale = 1.0 / math.sqrt(members)
    rows_x = weights(NX, 0, NXC, 0)
    rows_y = weights(NY, 0, NYC, 0)
    smooth = alpha
    for step in range(PASSES):
        smooth = one_pass(smooth)

    def accumulate(total, item):
        coarse_one, pert = item
        part = jnp.einsum('ia,lab->lib', rows_x, coarse_one, precision=highest)
        fine = jnp.einsum('lib,jb->lij', part, rows_y, precision=highest)
        return (total + fine[None] * pert.astype(jnp.float32), None)
    total, _ = lax.scan(accumulate, jnp.zeros((2, LEV, NX, NY), jnp.float32), (smooth, perturbation))
    increment = total * scale
    padded = jnp.pad(increment, ((0, 0), (0, 0), (1, 1), (1, 1)))
    zonal_x, zonal_y = slopes(padded[0])
    merid_x, _ = slopes(padded[1])
    zonal = increment[0]
    merid = increment[1]
    fields = jnp.stack([zonal, merid, merid_x - zonal_y, zonal * zonal_x + merid * zonal_y])
    region = (jnp.arange(OBS) // OBS_REG).astype(jnp.int32)
    level = obs_cell // (RX * NY)
    rest = obs_cell % (RX * NY)
    row_in = rest // NY
    column = rest % NY
    flat = obs_kind * (LEV * NX * NY) + level * (NX * NY) + (region * RX + row_in) * NY + column
    seen = fields.reshape(-1)[flat]
    misfit = obs_weight * (seen - obs_value)
    adjoint = jax.ops.segment_sum(misfit, flat, num_segments=4 * LEV * NX * NY).reshape(4, LEV, NX, NY)
    carried = jnp.stack([adjoint[2], adjoint[3] * zonal, adjoint[3] * merid])
    back = jnp.pad(carried, ((0, 0), (0, 0), (1, 1), (1, 1)))
    vort_x, vort_y = slopes(back[0])
    flux_x, _ = slopes(back[1])
    _, flux_y = slopes(back[2])
    grad_u = adjoint[0] + adjoint[3] * zonal_x + vort_y - flux_x - flux_y
    grad_v = adjoint[1] + adjoint[3] * zonal_y - vort_x
    grad_fine = jnp.stack([grad_u, grad_v])

    def project(pert):
        product = lax.optimization_barrier(jnp.sum(pert.astype(jnp.float32) * grad_fine, axis=0))
        part = jnp.einsum('lij,jb->lib', product, rows_y, precision=highest)
        return jnp.einsum('ia,lib->lab', rows_x, part, precision=highest) * scale
    gradient = lax.map(project, perturbation)
    for step in range(PASSES):
        gradient = one_pass(gradient)
    return gradient
```

```python
import functools
import math

import jax
import jax.numpy as jnp
from jax import lax
from jax.experimental import pallas as pl
from jax.experimental.pallas import tpu as pltpu
from jax.sharding import PartitionSpec as P

PASSES = 2
HALO = PASSES + 1
DIFFUSE = 0.2
F32 = jnp.float32
BF16 = jnp.bfloat16


def params(mib):
    return pltpu.CompilerParams(vmem_limit_bytes=mib << 20)


def swap_pairs(n, odd):
    pairs = []
    for i in range(1 if odd else 0, n - 1, 2):
        pairs += [(i, i + 1), (i + 1, i)]
    return pairs


def swap_even(value):
    return lax.ppermute(value, "reg", swap_pairs(lax.axis_size("reg"), False))


def swap_odd(value):
    return lax.ppermute(value, "reg", swap_pairs(lax.axis_size("reg"), True))


def others(value, axis):
    n = lax.axis_size(axis)
    stride = 1
    rounds = []
    while stride < n:
        left = n // stride
        radix = 4 if left % 4 == 0 else 2 if left % 2 == 0 else left
        sends = []
        for k in range(1, radix):
            pairs = []
            for i in range(n):
                digit = (i // stride) % radix
                other = digit ^ k if radix in (2, 4) else (digit + k) % radix
                pairs.append((i, i + (other - digit) * stride))
            sends.append(pairs)
        rounds.append(sends)
        stride *= radix
    for number, sends in enumerate(rounds):
        got = [lax.ppermute(value, axis, pairs) for pairs in sends]
        if number == len(rounds) - 1:
            return [value] + got
        for part in got:
            value = value + part
    return [value]


def split(x):
    high = x.astype(BF16)
    return high, (x - high.astype(F32)).astype(BF16)


def dot_nn(a, b):
    return lax.dot_general(a, b, (((1,), (0,)), ((), ())), preferred_element_type=F32)


def dot_nt(a, b):
    return lax.dot_general(a, b, (((1,), (1,)), ((), ())), preferred_element_type=F32)


def iota(shape, dim):
    return lax.broadcasted_iota(jnp.int32, shape, dim)


def table_y(coarse, fine, coarse_dim):
    shape = (coarse, fine) if coarse_dim == 0 else (fine, coarse)
    ratio = fine // coarse
    at = (iota(shape, 1 - coarse_dim).astype(F32) + 0.5) / ratio - 0.5
    return jnp.maximum(0.0, 1.0 - jnp.abs(at - iota(shape, coarse_dim).astype(F32))).astype(BF16)


def weights_x(i, ratio):
    at = (i + 0.5) / ratio - 0.5
    low = math.floor(at)
    return low, 1.0 - (at - low), at - low


def one_pass(rows, index, columns):
    mid = rows.get(index)
    around = None
    if mid is not None:
        lane = iota(mid.shape, 1)
        left = jnp.where(lane == 0, 0.0, pltpu.roll(mid, 1, 1))
        right = jnp.where(lane == columns - 1, 0.0, pltpu.roll(mid, columns - 1, 1))
        around = left + right
    for near in (index + 1, index - 1):
        if near in rows:
            around = rows[near] if around is None else around + rows[near]
    if mid is None:
        return DIFFUSE * around
    return mid + DIFFUSE * (around - 4.0 * mid)


def mask_row(value, index, coarse_rows, region, regions):
    if index < 0:
        return jnp.where(region * coarse_rows + index >= 0, value, 0.0)
    if index >= coarse_rows:
        return jnp.where(region * coarse_rows + index < regions * coarse_rows, value, 0.0)
    return value


def pack_kernel(pert_ref, a_ref, b_ref):
    even = lax.rem(lax.axis_index("reg"), 2) == 0
    block = pert_ref[0].astype(F32)
    first = block[:, :, 0, :]
    last = block[:, :, block.shape[2] - 1, :]
    a_ref[0] = jnp.where(even, last, first)
    b_ref[0] = jnp.where(even, first, last)


def pack(pert):
    members, parts, levels, rows, columns = pert.shape
    out = jax.ShapeDtypeStruct((members, parts, levels, columns), F32)
    spec = pl.BlockSpec((1, parts, levels, columns), lambda m: (m, 0, 0, 0))
    return pl.pallas_call(
        pack_kernel,
        grid=(members,),
        in_specs=[pl.BlockSpec((1, parts, levels, rows, columns), lambda m: (m, 0, 0, 0, 0))],
        out_specs=[spec, spec],
        out_shape=[out, out],
        compiler_params=params(16),
        name="pack_rows",
    )(pert)


def decode(cell, rows, columns):
    plane = rows * columns
    level = cell // plane
    rest = cell - level * plane
    row = rest // columns
    return level, row, rest - row * columns


def tables_kernel(levels, rows, columns, cell_ref, kind_ref, r0_ref, ru_ref, rv_ref, c0_ref, cy_ref):
    cell, kind = cell_ref[...], kind_ref[...]
    level, row, column = decode(cell, rows, columns)
    line = level * rows + row
    count = cell.shape[1]
    inner = levels * rows
    above = jnp.where(row > 0, line - 1, -1)
    below = jnp.where(row < rows - 1, line + 1, -1)
    up_edge = jnp.where(row == 0, inner + level, -1)
    down_edge = jnp.where(row == rows - 1, inner + levels + level, -1)
    minus = jnp.where(row > 0, above, up_edge)
    plus = jnp.where(row < rows - 1, below, down_edge)
    none = jnp.full_like(line, -1)
    here_u = line
    minus_u = jnp.where(kind == 3, minus, none)
    plus_u = jnp.where(kind == 3, plus, none)
    here_v = jnp.where((kind == 1) | (kind == 3), line, none)
    minus_v = jnp.where(kind == 2, minus, none)
    plus_v = jnp.where(kind == 2, plus, none)
    step = 32

    def lines(k, _):
        start = pl.multiple_of(k * step, step)
        at = iota((step, count), 0) + start
        ru = jnp.where(at == plus_u, 0.5, jnp.where(at == minus_u, -0.5, 0.0))
        rv = jnp.where(at == plus_v, 0.5, jnp.where(at == minus_v, -0.5, jnp.where(at == here_v, 1.0, 0.0)))
        r0 = jnp.where(at == here_u, 1.0, 0.0)
        ru_ref[pl.ds(start, step), :] = ru.astype(BF16)
        rv_ref[pl.ds(start, step), :] = rv.astype(BF16)
        r0_ref[pl.ds(start, step), :] = r0.astype(BF16)
        return 0

    lax.fori_loop(0, (inner + 2 * levels) // step, lines, 0)

    def cells(k, _):
        start = pl.multiple_of(k * step, step)
        at = iota((step, count), 0) + start
        c0_ref[pl.ds(start, step), :] = jnp.where(at == column, 1.0, 0.0).astype(BF16)
        cy = jnp.where(at == column + 1, 0.5, jnp.where(at == column - 1, -0.5, 0.0))
        cy_ref[pl.ds(start, step), :] = cy.astype(BF16)
        return 0

    lax.fori_loop(0, columns // step, cells, 0)


def tables(cell, kind, levels, rows, columns):
    count = cell.shape[1]
    lines = levels * rows + 2 * levels
    shapes = [jax.ShapeDtypeStruct((n, count), BF16) for n in (lines, lines, lines, columns, columns)]
    return pl.pallas_call(
        functools.partial(tables_kernel, levels, rows, columns),
        out_shape=shapes,
        compiler_params=params(16),
        name="one_hots",
    )(cell, kind)


def forward_kernel(
    scale, members, levels, chunk, coarse_rows, rows,
    own_ref, even_ref, odd_ref, pert_ref, r0_ref, ru_ref, rv_ref, c0_ref, cy_ref,
    q_ref, edge_ref,
    fine_in, fine_scr, u_scr, v_scr, ty_scr, t_scr,
):
    step = pl.program_id(0)
    steps = pl.num_programs(0)
    region = lax.axis_index("reg")
    regions = lax.axis_size("reg")
    pairs = members * levels
    coarse_columns = own_ref.shape[1]
    columns = u_scr.shape[1]
    ratio = rows // coarse_rows
    block = chunk * rows

    @pl.when(step == 0)
    def _():
        even = lax.rem(region, 2) == 0
        table = table_y(coarse_columns, columns, 0)
        ty_scr[pl.ds(0, coarse_columns), :] = table
        ty_scr[pl.ds(coarse_columns, coarse_columns), :] = table
        rows_in = {}
        for r in range(coarse_rows):
            rows_in[r] = own_ref[pl.ds(r, pairs, stride=coarse_rows), :]
        for k in range(HALO):
            low = coarse_rows - HALO + k
            e = even_ref[pl.ds(low, pairs, stride=coarse_rows), :]
            o = odd_ref[pl.ds(low, pairs, stride=coarse_rows), :]
            rows_in[k - HALO] = jnp.where(even, o, e)
            e = even_ref[pl.ds(k, pairs, stride=coarse_rows), :]
            o = odd_ref[pl.ds(k, pairs, stride=coarse_rows), :]
            rows_in[coarse_rows + k] = jnp.where(even, e, o)
        for done in range(PASSES):
            reach = HALO - 1 - done
            rows_in = {
                r: mask_row(one_pass(rows_in, r, coarse_columns), r, coarse_rows, region, regions)
                for r in range(-reach, coarse_rows + reach)
            }
        for i in range(-1, rows + 1):
            low, w0, w1 = weights_x(i, ratio)
            value = (w0 * rows_in[low] + w1 * rows_in[low + 1]) * scale
            if 0 <= i < rows:
                fine_in[pl.ds(i, pairs, stride=rows), :] = value
            else:
                high, lower = split(value)
                got = dot_nn(jnp.concatenate([high, lower], axis=1), ty_scr[...])
                edge_ref[0 if i < 0 else 1] = got

    parts = []
    for m in range(members):
        start = pl.multiple_of(m * levels * rows + step * block, block)
        parts.append(fine_in[pl.ds(start, block), :])
    high, lower = split(jnp.concatenate(parts, axis=0))
    fine_scr[...] = dot_nn(jnp.concatenate([high, lower], axis=1), ty_scr[...])
    base = step * block

    def level(k, _):
        at = pl.multiple_of(k * rows, rows)
        u = v = None
        for m in range(members):
            fine = fine_scr[pl.ds(m * block + at, rows), :]
            pu = fine * pert_ref[m, 0, k].astype(F32)
            pv = fine * pert_ref[m, 1, k].astype(F32)
            u = pu if u is None else u + pu
            v = pv if v is None else v + pv
        to = pl.multiple_of(base + at, rows)
        u_scr[pl.ds(to, rows), :] = u
        v_scr[pl.ds(to, rows), :] = v
        return 0

    lax.fori_loop(0, chunk, level, 0)

    @pl.when(step == steps - 1)
    def _():
        inner = levels * rows
        for n, source in enumerate((u_scr, v_scr)):
            high, lower = split(source[...].T)
            t_scr[2 * n] = high
            t_scr[2 * n + 1] = lower
        count = r0_ref.shape[1]
        width = min(256, count)

        def observe(k, _):
            at = pl.ds(pl.multiple_of(k * width, width), width)
            c0 = c0_ref[:, at].astype(F32)
            cy = cy_ref[:, at].astype(F32)
            r0 = r0_ref[pl.ds(0, inner), at]
            u_row = dot_nn(t_scr[0], r0) + dot_nn(t_scr[1], r0)
            q_ref[pl.ds(0, 1), at] = jnp.sum(u_row * c0, axis=0, keepdims=True)
            q_ref[pl.ds(3, 1), at] = jnp.sum(u_row * cy, axis=0, keepdims=True)
            rv = rv_ref[pl.ds(0, inner), at]
            v_row = dot_nn(t_scr[2], rv) + dot_nn(t_scr[3], rv)
            q_ref[pl.ds(1, 1), at] = jnp.sum(v_row * c0, axis=0, keepdims=True)
            ru = ru_ref[pl.ds(0, inner), at]
            d_row = dot_nn(t_scr[0], ru) + dot_nn(t_scr[1], ru)
            q_ref[pl.ds(2, 1), at] = jnp.sum(d_row * c0, axis=0, keepdims=True)
            return 0

        lax.fori_loop(0, count // width, observe, 0)


def forward(own, got_even, got_odd, pert, hot, scale):
    members, parts, levels, rows, columns = pert.shape
    pairs = members * levels
    coarse_rows = own.shape[0] // pairs
    coarse_columns = own.shape[1]
    chunk = 4 if levels % 4 == 0 else 1
    count = hot[0].shape[1]
    whole = lambda x: pl.BlockSpec(x.shape, lambda s: (0,) * x.ndim)
    return pl.pallas_call(
        functools.partial(forward_kernel, scale, members, levels, chunk, coarse_rows, rows),
        grid=(levels // chunk,),
        in_specs=[whole(own), whole(own), whole(own),
                  pl.BlockSpec((members, parts, chunk, rows, columns), lambda s: (0, 0, s, 0, 0)),
                  *[whole(h) for h in hot]],
        out_specs=[pl.BlockSpec((4, count), lambda s: (0, 0)),
                   pl.BlockSpec((2, pairs, columns), lambda s: (0, 0, 0))],
        out_shape=[jax.ShapeDtypeStruct((4, count), F32),
                   jax.ShapeDtypeStruct((2, pairs, columns), F32)],
        scratch_shapes=[
            pltpu.VMEM((pairs * rows, coarse_columns), F32),
            pltpu.VMEM((members * chunk * rows, columns), F32),
            pltpu.VMEM((levels * rows, columns), F32),
            pltpu.VMEM((levels * rows, columns), F32),
            pltpu.VMEM((2 * coarse_columns, columns), BF16),
            pltpu.VMEM((4, columns, levels * rows), BF16),
        ],
        compiler_params=params(40),
        name="increment_at_obs",
    )(own, got_even, got_odd, pert, *hot)


def edge_kernel(members, levels, q_ref, fine_ref, even_ref, odd_ref, ru_ref, rv_ref, c0_ref, out_ref):
    even = lax.rem(lax.axis_index("reg"), 2) == 0
    columns = fine_ref.shape[2]
    table = []
    for part in range(2):
        for side in range(2):
            total = None
            for m in range(members):
                e, o = even_ref[m, part], odd_ref[m, part]
                halo = jnp.where(even, o, e) if side == 0 else jnp.where(even, e, o)
                term = fine_ref[side, pl.ds(m * levels, levels), :] * halo
                total = term if total is None else total + term
            table.append(total)
    u = jnp.concatenate(table[:2], axis=0).T
    v = jnp.concatenate(table[2:], axis=0).T
    u_high, u_low = split(u)
    v_high, v_low = split(v)
    left = jnp.concatenate([u_high, u_low, v_high, v_low], axis=1)
    ru, rv = ru_ref[...], rv_ref[...]
    count = ru.shape[1]
    width = min(256, count)
    for k in range(count // width):
        at = pl.ds(k * width, width)
        rc = ru_ref[:, at]
        vc = rv_ref[:, at]
        row = dot_nn(left, jnp.concatenate([rc, rc, vc, vc], axis=0))
        seen = jnp.sum(row * c0_ref[:, at].astype(F32), axis=0, keepdims=True)
        in_u = jnp.sum(jnp.abs(rc.astype(F32)), axis=0, keepdims=True) > 0.0
        in_v = jnp.sum(jnp.abs(vc.astype(F32)), axis=0, keepdims=True) > 0.0
        out_ref[pl.ds(0, 1), at] = q_ref[pl.ds(0, 1), at]
        out_ref[pl.ds(1, 1), at] = q_ref[pl.ds(1, 1), at] + jnp.where(in_v, seen, 0.0)
        out_ref[pl.ds(2, 1), at] = q_ref[pl.ds(2, 1), at] + jnp.where(in_u, seen, 0.0)
        out_ref[pl.ds(3, 1), at] = q_ref[pl.ds(3, 1), at]


def edge(q, fine, halo_even, halo_odd, hot, members, levels):
    _, ru, rv, c0, _ = hot
    lines, count = ru.shape
    tail = 2 * levels
    whole = lambda x: pl.BlockSpec(x.shape, lambda s: (0,) * x.ndim)
    last = pl.BlockSpec((tail, count), lambda s: (lines // tail - 1, 0))
    return pl.pallas_call(
        functools.partial(edge_kernel, members, levels),
        grid=(1,),
        in_specs=[whole(q), whole(fine), whole(halo_even), whole(halo_odd), last, last, whole(c0)],
        out_specs=whole(q),
        out_shape=jax.ShapeDtypeStruct(q.shape, F32),
        compiler_params=params(24),
        name="edge_at_obs",
    )(q, fine, halo_even, halo_odd, ru, rv, c0)


def backward_kernel(
    scale, members, levels, chunk, coarse_rows, rows, terms,
    *refs,
):
    q_refs = refs[:terms]
    (kind_ref, value_ref, weight_ref, pert_ref, even_ref, odd_ref,
     r0_ref, ru_ref, rv_ref, c0_ref, cy_ref,
     own_out, a_out, b_out,
     u_scr, v_scr, ty_scr, f_scr) = refs[terms:]
    step = pl.program_id(0)
    steps = pl.num_programs(0)
    region = lax.axis_index("reg")
    regions = lax.axis_size("reg")
    pairs = members * levels
    columns, coarse_columns = ty_scr.shape
    ratio = rows // coarse_rows
    block = chunk * rows
    inner = levels * rows
    even = lax.rem(region, 2) == 0

    @pl.when(step == 0)
    def _():
        ty_scr[...] = table_y(coarse_columns, columns, 1)
        q = q_refs[0][...]
        for ref in q_refs[1:]:
            q = q + ref[...]
        q0, q1, q2, q3 = (q[n : n + 1] for n in range(4))
        kind = kind_ref[...]
        seen = jnp.where(kind == 0, q0, jnp.where(kind == 1, q1, jnp.where(kind == 2, q1 - q3, q0 * q2 + q1 * q3)))
        misfit = weight_ref[...] * (seen - value_ref[...])
        zero = jnp.zeros_like(misfit)
        a = jnp.where(kind == 0, misfit, jnp.where(kind == 3, misfit * q2, zero))
        b = jnp.where(kind == 2, -misfit, jnp.where(kind == 3, misfit * q1, zero))
        c = jnp.where(kind == 3, misfit * q0, zero)
        g = jnp.where(kind == 3, misfit * q3, jnp.where(kind == 0, zero, misfit))
        c0, cy = c0_ref[...], cy_ref[...]
        r0, ru, rv = r0_ref[pl.ds(0, inner), :], ru_ref[...], rv_ref[...]
        total_u = total_c = total_v = None
        for a_part, b_part, c_part, g_part in zip(split(a), split(b), split(c), split(g)):
            t = dot_nt(r0, c0 * a_part + cy * b_part)
            total_u = t if total_u is None else total_u + t
            t = dot_nt(ru, c0 * c_part)
            total_c = t if total_c is None else total_c + t
            t = dot_nt(rv, c0 * g_part)
            total_v = t if total_v is None else total_v + t
        u_scr[pl.ds(0, inner), :] = total_u + total_c[:inner]
        u_scr[pl.ds(inner, 2 * levels), :] = total_c[inner:]
        v_scr[...] = total_v

    def level(k, _):
        at = pl.multiple_of(k * rows, rows)
        here = pl.multiple_of(step * block + at, rows)
        u = u_scr[pl.ds(here, rows), :]
        v = v_scr[pl.ds(here, rows), :]
        product = [u * pert_ref[m, 0, k].astype(F32) + v * pert_ref[m, 1, k].astype(F32) for m in range(members)]
        high, lower = split(jnp.concatenate(product, axis=0))
        got = dot_nn(high, ty_scr[...]) + dot_nn(lower, ty_scr[...])
        for m in range(members):
            to = pl.multiple_of(m * inner + here, rows)
            f_scr[pl.ds(to, rows), :] = got[m * rows : (m + 1) * rows]
        return 0

    lax.fori_loop(0, chunk, level, 0)

    @pl.when(step == steps - 1)
    def _():
        out = {}

        def add(i, value):
            low, w0, w1 = weights_x(i, ratio)
            for at, w in ((low, w0), (low + 1, w1)):
                out[at] = w * value if at not in out else out[at] + w * value

        for side in range(2):
            u = u_scr[pl.ds(inner + side * levels, levels), :]
            v = v_scr[pl.ds(inner + side * levels, levels), :]
            product = []
            for m in range(members):
                halo = []
                for part in range(2):
                    e, o = even_ref[m, part], odd_ref[m, part]
                    halo.append(jnp.where(even, o, e) if side == 0 else jnp.where(even, e, o))
                product.append(u * halo[0] + v * halo[1])
            high, lower = split(jnp.concatenate(product, axis=0))
            got = dot_nn(high, ty_scr[...]) + dot_nn(lower, ty_scr[...])
            add(-1 if side == 0 else rows, got)
        for i in range(rows):
            add(i, f_scr[pl.ds(i, pairs, stride=rows), :])
        held = {r: mask_row(value * scale, r, coarse_rows, region, regions) for r, value in out.items()}
        for done in range(PASSES):
            reach = 2 + done
            held = {
                r: mask_row(one_pass(held, r, coarse_columns), r, coarse_rows, region, regions)
                for r in range(-reach, coarse_rows + reach)
            }
        for r in range(coarse_rows):
            own_out[r] = held[r]
        for k in range(HALO):
            before, after = held[k - HALO], held[coarse_rows + k]
            a_out[k] = jnp.where(even, after, before)
            b_out[k] = jnp.where(even, before, after)


def backward(q_terms, kind, value, weight, pert, halo_even, halo_odd, hot, scale, coarse_rows, coarse_columns):
    members, parts, levels, rows, columns = pert.shape
    pairs = members * levels
    chunk = 4 if levels % 4 == 0 else 1
    whole = lambda x: pl.BlockSpec(x.shape, lambda s: (0,) * len(x.shape))
    outs = [jax.ShapeDtypeStruct((n, pairs, coarse_columns), F32) for n in (coarse_rows, HALO, HALO)]
    return pl.pallas_call(
        functools.partial(backward_kernel, scale, members, levels, chunk, coarse_rows, rows, len(q_terms)),
        grid=(levels // chunk,),
        in_specs=[*[whole(q) for q in q_terms], whole(kind), whole(value), whole(weight),
                  pl.BlockSpec((members, parts, chunk, rows, columns), lambda s: (0, 0, s, 0, 0)),
                  whole(halo_even), whole(halo_odd), *[whole(h) for h in hot]],
        out_specs=[whole(o) for o in outs],
        out_shape=outs,
        scratch_shapes=[
            pltpu.VMEM((levels * rows + 2 * levels, columns), F32),
            pltpu.VMEM((levels * rows + 2 * levels, columns), F32),
            pltpu.VMEM((columns, coarse_columns), BF16),
            pltpu.VMEM((pairs * rows, coarse_columns), F32),
        ],
        compiler_params=params(40),
        name="adjoint_to_coarse",
    )(*q_terms, kind, value, weight, pert, halo_even, halo_odd, *hot)


def join_kernel(coarse_rows, own_ref, even_ref, odd_ref, out_ref):
    even = lax.rem(lax.axis_index("reg"), 2) == 0
    pairs = own_ref.shape[1]
    for r in range(coarse_rows):
        total = own_ref[r]
        if r < HALO:
            total = total + jnp.where(even, odd_ref[r], even_ref[r])
        k = r - (coarse_rows - HALO)
        if k >= 0:
            total = total + jnp.where(even, even_ref[k], odd_ref[k])
        out_ref[pl.ds(r, pairs, stride=coarse_rows), :] = total


def join(own, got_even, got_odd):
    coarse_rows, pairs, columns = own.shape
    return pl.pallas_call(
        functools.partial(join_kernel, coarse_rows),
        out_shape=jax.ShapeDtypeStruct((pairs * coarse_rows, columns), F32),
        compiler_params=params(16),
        name="join_rows",
    )(own, got_even, got_odd)


def local(alpha, perturbation, obs_cell, obs_kind, obs_value, obs_weight):
    members, levels, coarse_rows, coarse_columns = alpha.shape
    _, _, _, rows, columns = perturbation.shape
    scale = 1.0 / math.sqrt(members * lax.axis_size("mem"))
    flat = alpha.reshape(-1, coarse_columns)
    flat_even, flat_odd = swap_even(flat), swap_odd(flat)
    pack_a, pack_b = pack(perturbation)
    halo_even, halo_odd = swap_even(pack_a), swap_odd(pack_b)
    cell, kind, value, weight = (x.reshape(1, -1) for x in (obs_cell, obs_kind, obs_value, obs_weight))
    hot = tables(cell, kind, levels, rows, columns)
    q, edge_fine = forward(flat, flat_even, flat_odd, perturbation, hot, scale)
    q = edge(q, edge_fine, halo_even, halo_odd, hot, members, levels)
    own, send_a, send_b = backward(
        others(q, "mem"), kind, value, weight, perturbation, halo_even, halo_odd, hot, scale,
        coarse_rows, coarse_columns,
    )
    return join(own, swap_even(send_a), swap_odd(send_b)).reshape(alpha.shape)


def solution(mesh):
    return jax.shard_map(
        local,
        mesh=mesh,
        in_specs=(
            P("mem", None, "reg", None),
            P("mem", None, None, "reg", None),
            P("reg"),
            P("reg"),
            P("reg"),
            P("reg"),
        ),
        out_specs=P("mem", None, "reg", None),
        check_vma=False,
    )
```

```python
import functools
import math

import jax
import jax.numpy as jnp
from jax import lax
from jax.experimental import pallas as pl
from jax.experimental.pallas import tpu as pltpu
from jax.sharding import PartitionSpec as P


PASSES = 2
HALO = PASSES + 1
DIFFUSE = 0.2
F32 = jnp.float32
BF16 = jnp.bfloat16


def params(mib):
    return pltpu.CompilerParams(vmem_limit_bytes=mib << 20)


def swap_pairs(n, odd):
    pairs = []
    for i in range(1 if odd else 0, n - 1, 2):
        pairs += [(i, i + 1), (i + 1, i)]
    return pairs


def swap_even(value):
    return lax.ppermute(value, "reg", swap_pairs(lax.axis_size("reg"), False))


def swap_odd(value):
    return lax.ppermute(value, "reg", swap_pairs(lax.axis_size("reg"), True))


def others(value, axis):
    n = lax.axis_size(axis)
    stride = 1
    rounds = []
    while stride < n:
        left = n // stride
        radix = 4 if left % 4 == 0 else 2 if left % 2 == 0 else left
        sends = []
        for k in range(1, radix):
            pairs = []
            for i in range(n):
                digit = (i // stride) % radix
                other = digit ^ k if radix in (2, 4) else (digit + k) % radix
                pairs.append((i, i + (other - digit) * stride))
            sends.append(pairs)
        rounds.append(sends)
        stride *= radix
    for number, sends in enumerate(rounds):
        got = [lax.ppermute(value, axis, pairs) for pairs in sends]
        if number == len(rounds) - 1:
            return [value] + got
        for part in got:
            value = value + part
    return [value]


def split(x):
    high = x.astype(BF16)
    return high, (x - high.astype(F32)).astype(BF16)


def dot_nn(a, b):
    return lax.dot_general(a, b, (((1,), (0,)), ((), ())), preferred_element_type=F32)


def dot_nt(a, b):
    return lax.dot_general(a, b, (((1,), (1,)), ((), ())), preferred_element_type=F32)


def iota(shape, dim):
    return lax.broadcasted_iota(jnp.int32, shape, dim)


def table_y(coarse, fine, coarse_dim):
    shape = (coarse, fine) if coarse_dim == 0 else (fine, coarse)
    ratio = fine // coarse
    at = (iota(shape, 1 - coarse_dim).astype(F32) + 0.5) / ratio - 0.5
    return jnp.maximum(0.0, 1.0 - jnp.abs(at - iota(shape, coarse_dim).astype(F32))).astype(BF16)


def weights_x(i, ratio):
    at = (i + 0.5) / ratio - 0.5
    low = math.floor(at)
    return low, 1.0 - (at - low), at - low


def one_pass(rows, index, columns):
    mid = rows.get(index)
    around = None
    if mid is not None:
        lane = iota(mid.shape, 1)
        left = jnp.where(lane == 0, 0.0, pltpu.roll(mid, 1, 1))
        right = jnp.where(lane == columns - 1, 0.0, pltpu.roll(mid, columns - 1, 1))
        around = left + right
    for near in (index + 1, index - 1):
        if near in rows:
            around = rows[near] if around is None else around + rows[near]
    if mid is None:
        return DIFFUSE * around
    return mid + DIFFUSE * (around - 4.0 * mid)


def mask_row(value, index, coarse_rows, region, regions):
    if index < 0:
        return jnp.where(region * coarse_rows + index >= 0, value, 0.0)
    if index >= coarse_rows:
        return jnp.where(region * coarse_rows + index < regions * coarse_rows, value, 0.0)
    return value


def decode(cell, rows, columns):
    plane = rows * columns
    level = cell // plane
    rest = cell - level * plane
    row = rest // columns
    return level, row, rest - row * columns


def prepare_kernel(
    pert_hbm, cell_hbm, kind_hbm, flat_hbm,
    pert_ref, a_ref, b_ref, r0_ref, ru_ref, rv_ref, c0_ref, cy_ref, own_ref,
    cell_ref, kind_ref, flat_ref, sem, small_sem,
):
    members, parts, levels, rows, columns = pert_ref.shape
    small = []
    for n, (source, to) in enumerate(((cell_hbm, cell_ref), (kind_hbm, kind_ref), (flat_hbm, flat_ref))):
        copy = pltpu.make_async_copy(source, to, small_sem.at[n])
        copy.start()
        small.append(copy)
    copies = []
    for m in range(members):
        copy = pltpu.make_async_copy(pert_hbm.at[m], pert_ref.at[m], sem.at[m])
        copy.start()
        copies.append(copy)

    small[0].wait()
    small[1].wait()
    cell, kind = cell_ref[...], kind_ref[...]
    level, row, column = decode(cell, rows, columns)
    line = level * rows + row
    count = cell.shape[1]
    inner = levels * rows
    minus = jnp.where(row > 0, line - 1, inner + level)
    plus = jnp.where(row < rows - 1, line + 1, inner + levels + level)
    none = jnp.full_like(line, -1)
    minus_u = jnp.where(kind == 3, minus, none)
    plus_u = jnp.where(kind == 3, plus, none)
    here_v = jnp.where((kind == 1) | (kind == 3), line, none)
    minus_v = jnp.where(kind == 2, minus, none)
    plus_v = jnp.where(kind == 2, plus, none)
    step = 32

    def lines(k, _):
        start = pl.multiple_of(k * step, step)
        at = iota((step, count), 0) + start
        ru = jnp.where(at == plus_u, 0.5, jnp.where(at == minus_u, -0.5, 0.0))
        rv = jnp.where(at == plus_v, 0.5, jnp.where(at == minus_v, -0.5, jnp.where(at == here_v, 1.0, 0.0)))
        r0 = jnp.where(at == line, 1.0, 0.0)
        ru_ref[pl.ds(start, step), :] = ru.astype(BF16)
        rv_ref[pl.ds(start, step), :] = rv.astype(BF16)
        r0_ref[pl.ds(start, step), :] = r0.astype(BF16)
        return 0

    lax.fori_loop(0, (inner + 2 * levels) // step, lines, 0)

    def cells(k, _):
        start = pl.multiple_of(k * step, step)
        at = iota((step, count), 0) + start
        c0_ref[pl.ds(start, step), :] = jnp.where(at == column, 1.0, 0.0).astype(BF16)
        cy = jnp.where(at == column + 1, 0.5, jnp.where(at == column - 1, -0.5, 0.0))
        cy_ref[pl.ds(start, step), :] = cy.astype(BF16)
        return 0

    lax.fori_loop(0, columns // step, cells, 0)

    coarse_rows, pairs, _ = own_ref.shape
    small[2].wait()
    for r in range(coarse_rows):
        own_ref[r] = flat_ref[pl.ds(r, pairs, stride=coarse_rows), :]

    even = lax.rem(lax.axis_index("reg"), 2) == 0
    shape = (2 * levels, inner)
    pick = iota(shape, 0)
    to_a = pick < levels
    edge = jnp.where(to_a == even, rows - 1, 0)
    wanted = jnp.where(to_a, pick, pick - levels) * rows + edge
    chooser = jnp.where(iota(shape, 1) == wanted, 1.0, 0.0).astype(BF16)
    for m in range(members):
        copies[m].wait()
        for part in range(parts):
            got = dot_nn(chooser, pert_ref[m, part].reshape(inner, columns))
            a_ref[m, part] = got[:levels]
            b_ref[m, part] = got[levels:]


def prepare(pert, cell, kind, flat, coarse_rows):
    members, parts, levels, rows, columns = pert.shape
    count = cell.shape[1]
    lines = levels * rows + 2 * levels
    shapes = [jax.ShapeDtypeStruct(pert.shape, pert.dtype)]
    shapes += [jax.ShapeDtypeStruct((members, parts, levels, columns), F32)] * 2
    shapes += [jax.ShapeDtypeStruct((n, count), BF16) for n in (lines, lines, lines, columns, columns)]
    shapes.append(jax.ShapeDtypeStruct((coarse_rows, flat.shape[0] // coarse_rows, flat.shape[1]), F32))
    vmem = pl.BlockSpec(memory_space=pltpu.VMEM)
    hbm = pl.BlockSpec(memory_space=pltpu.HBM)
    pert, cell, kind, flat = (pltpu.with_memory_space_constraint(x, pltpu.HBM) for x in (pert, cell, kind, flat))
    held, pack_a, pack_b, *hot, own = pl.pallas_call(
        prepare_kernel,
        in_specs=[hbm] * 4,
        out_specs=[vmem] * len(shapes),
        out_shape=shapes,
        scratch_shapes=[
            pltpu.VMEM(cell.shape, cell.dtype),
            pltpu.VMEM(kind.shape, kind.dtype),
            pltpu.VMEM(flat.shape, flat.dtype),
            pltpu.SemaphoreType.DMA((members,)),
            pltpu.SemaphoreType.DMA((3,)),
        ],
        compiler_params=params(16),
        name="prepare",
    )(pert, cell, kind, flat)
    return held, pack_a, pack_b, hot, own


def forward_kernel(
    scale, chunk,
    own_ref, even_ref, odd_ref, pert_ref, r0_ref, ru_ref, rv_ref, c0_ref, cy_ref,
    q_ref, edge_ref,
    fine_in, fine_scr, u_scr, v_scr, t_scr,
):
    region = lax.axis_index("reg")
    regions = lax.axis_size("reg")
    members, _, levels, rows, columns = pert_ref.shape
    coarse_rows, pairs, coarse_columns = own_ref.shape
    ratio = rows // coarse_rows
    block = chunk * rows
    inner = levels * rows
    even = lax.rem(region, 2) == 0
    table = table_y(coarse_columns, columns, 0)
    table = jnp.concatenate([table, table], axis=0)

    rows_in = {r: own_ref[r] for r in range(coarse_rows)}
    for k in range(HALO):
        low = coarse_rows - HALO + k
        e = even_ref[pl.ds(low, pairs, stride=coarse_rows), :]
        o = odd_ref[pl.ds(low, pairs, stride=coarse_rows), :]
        rows_in[k - HALO] = jnp.where(even, o, e)
        e = even_ref[pl.ds(k, pairs, stride=coarse_rows), :]
        o = odd_ref[pl.ds(k, pairs, stride=coarse_rows), :]
        rows_in[coarse_rows + k] = jnp.where(even, e, o)
    for done in range(PASSES):
        reach = HALO - 1 - done
        rows_in = {
            r: mask_row(one_pass(rows_in, r, coarse_columns), r, coarse_rows, region, regions)
            for r in range(-reach, coarse_rows + reach)
        }
    for i in range(-1, rows + 1):
        low, w0, w1 = weights_x(i, ratio)
        value = (w0 * rows_in[low] + w1 * rows_in[low + 1]) * scale
        if 0 <= i < rows:
            fine_in[pl.ds(i, pairs, stride=rows), :] = value
        else:
            high, lower = split(value)
            got = dot_nn(jnp.concatenate([high, lower], axis=1), table)
            edge_ref[0 if i < 0 else 1] = got

    for step in range(levels // chunk):
        parts = []
        for m in range(members):
            parts.append(fine_in[pl.ds(m * inner + step * block, block), :])
        high, lower = split(jnp.concatenate(parts, axis=0))
        fine_scr[...] = dot_nn(jnp.concatenate([high, lower], axis=1), table)

        def level(k, _, step=step):
            at = pl.multiple_of(k * rows, rows)
            u = v = None
            for m in range(members):
                fine = fine_scr[pl.ds(m * block + at, rows), :]
                pu = fine * pert_ref[m, 0, step * chunk + k].astype(F32)
                pv = fine * pert_ref[m, 1, step * chunk + k].astype(F32)
                u = pu if u is None else u + pu
                v = pv if v is None else v + pv
            to = pl.multiple_of(step * block + at, rows)
            u_scr[pl.ds(to, rows), :] = u
            v_scr[pl.ds(to, rows), :] = v
            return 0

        lax.fori_loop(0, chunk, level, 0)

    for n, source in enumerate((u_scr, v_scr)):
        high, lower = split(source[...].T)
        t_scr[2 * n] = high
        t_scr[2 * n + 1] = lower
    count = r0_ref.shape[1]
    width = min(256, count)

    def observe(k, _):
        at = pl.ds(pl.multiple_of(k * width, width), width)
        c0 = c0_ref[:, at].astype(F32)
        cy = cy_ref[:, at].astype(F32)
        r0 = r0_ref[pl.ds(0, inner), at]
        u_row = dot_nn(t_scr[0], r0) + dot_nn(t_scr[1], r0)
        q_ref[pl.ds(0, 1), at] = jnp.sum(u_row * c0, axis=0, keepdims=True)
        q_ref[pl.ds(3, 1), at] = jnp.sum(u_row * cy, axis=0, keepdims=True)
        rv = rv_ref[pl.ds(0, inner), at]
        v_row = dot_nn(t_scr[2], rv) + dot_nn(t_scr[3], rv)
        q_ref[pl.ds(1, 1), at] = jnp.sum(v_row * c0, axis=0, keepdims=True)
        ru = ru_ref[pl.ds(0, inner), at]
        d_row = dot_nn(t_scr[0], ru) + dot_nn(t_scr[1], ru)
        q_ref[pl.ds(2, 1), at] = jnp.sum(d_row * c0, axis=0, keepdims=True)
        return 0

    lax.fori_loop(0, count // width, observe, 0)


def forward(own, got_even, got_odd, pert, hot, scale):
    members, _, levels, rows, columns = pert.shape
    _, pairs, coarse_columns = own.shape
    chunk = 4 if levels % 4 == 0 else 1
    count = hot[0].shape[1]
    return pl.pallas_call(
        functools.partial(forward_kernel, scale, chunk),
        out_shape=[jax.ShapeDtypeStruct((4, count), F32),
                   jax.ShapeDtypeStruct((2, pairs, columns), F32)],
        scratch_shapes=[
            pltpu.VMEM((pairs * rows, coarse_columns), F32),
            pltpu.VMEM((members * chunk * rows, columns), F32),
            pltpu.VMEM((levels * rows, columns), F32),
            pltpu.VMEM((levels * rows, columns), F32),
            pltpu.VMEM((4, columns, levels * rows), BF16),
        ],
        compiler_params=params(28),
        name="increment_at_obs",
    )(own, got_even, got_odd, pert, *hot)


def edge_kernel(members, levels, q_ref, fine_ref, even_ref, odd_ref, ru_ref, rv_ref, c0_ref, out_ref):
    even = lax.rem(lax.axis_index("reg"), 2) == 0
    table = []
    for part in range(2):
        for side in range(2):
            total = None
            for m in range(members):
                e, o = even_ref[m, part], odd_ref[m, part]
                halo = jnp.where(even, o, e) if side == 0 else jnp.where(even, e, o)
                term = fine_ref[side, pl.ds(m * levels, levels), :] * halo
                total = term if total is None else total + term
            table.append(total)
    u = jnp.concatenate(table[:2], axis=0).T
    v = jnp.concatenate(table[2:], axis=0).T
    u_high, u_low = split(u)
    v_high, v_low = split(v)
    left = jnp.concatenate([u_high, u_low, v_high, v_low], axis=1)
    lines, count = ru_ref.shape
    tail = pl.ds(lines - 2 * levels, 2 * levels)
    width = min(256, count)
    for k in range(count // width):
        at = pl.ds(k * width, width)
        rc = ru_ref[tail, at]
        vc = rv_ref[tail, at]
        row = dot_nn(left, jnp.concatenate([rc, rc, vc, vc], axis=0))
        seen = jnp.sum(row * c0_ref[:, at].astype(F32), axis=0, keepdims=True)
        in_u = jnp.sum(jnp.abs(rc.astype(F32)), axis=0, keepdims=True) > 0.0
        in_v = jnp.sum(jnp.abs(vc.astype(F32)), axis=0, keepdims=True) > 0.0
        out_ref[pl.ds(0, 1), at] = q_ref[pl.ds(0, 1), at]
        out_ref[pl.ds(1, 1), at] = q_ref[pl.ds(1, 1), at] + jnp.where(in_v, seen, 0.0)
        out_ref[pl.ds(2, 1), at] = q_ref[pl.ds(2, 1), at] + jnp.where(in_u, seen, 0.0)
        out_ref[pl.ds(3, 1), at] = q_ref[pl.ds(3, 1), at]


def edge(q, fine, halo_even, halo_odd, hot, members, levels):
    _, ru, rv, c0, _ = hot
    return pl.pallas_call(
        functools.partial(edge_kernel, members, levels),
        out_shape=jax.ShapeDtypeStruct(q.shape, F32),
        compiler_params=params(16),
        name="edge_at_obs",
    )(q, fine, halo_even, halo_odd, ru, rv, c0)


def backward_kernel(scale, chunk, terms, *refs):
    q_refs = refs[:terms]
    (kind_ref, value_ref, weight_ref, pert_ref, even_ref, odd_ref,
     r0_ref, ru_ref, rv_ref, c0_ref, cy_ref,
     own_out, a_out, b_out,
     u_scr, v_scr, f_scr) = refs[terms:]
    region = lax.axis_index("reg")
    regions = lax.axis_size("reg")
    members, _, levels, rows, columns = pert_ref.shape
    coarse_rows, pairs, coarse_columns = own_out.shape
    ratio = rows // coarse_rows
    inner = levels * rows
    even = lax.rem(region, 2) == 0
    table = table_y(coarse_columns, columns, 1)

    q = q_refs[0][...]
    for ref in q_refs[1:]:
        q = q + ref[...]
    q0, q1, q2, q3 = (q[n : n + 1] for n in range(4))
    kind = kind_ref[...]
    seen = jnp.where(kind == 0, q0, jnp.where(kind == 1, q1, jnp.where(kind == 2, q1 - q3, q0 * q2 + q1 * q3)))
    misfit = weight_ref[...] * (seen - value_ref[...])
    zero = jnp.zeros_like(misfit)
    a = jnp.where(kind == 0, misfit, jnp.where(kind == 3, misfit * q2, zero))
    b = jnp.where(kind == 2, -misfit, jnp.where(kind == 3, misfit * q1, zero))
    c = jnp.where(kind == 3, misfit * q0, zero)
    g = jnp.where(kind == 3, misfit * q3, jnp.where(kind == 0, zero, misfit))
    c0, cy = c0_ref[...], cy_ref[...]
    r0, ru, rv = r0_ref[pl.ds(0, inner), :], ru_ref[...], rv_ref[...]
    total_u = total_c = total_v = None
    for a_part, b_part, c_part, g_part in zip(split(a), split(b), split(c), split(g)):
        t = dot_nt(r0, c0 * a_part + cy * b_part)
        total_u = t if total_u is None else total_u + t
        t = dot_nt(ru, c0 * c_part)
        total_c = t if total_c is None else total_c + t
        t = dot_nt(rv, c0 * g_part)
        total_v = t if total_v is None else total_v + t
    u_scr[pl.ds(0, inner), :] = total_u + total_c[:inner]
    u_scr[pl.ds(inner, 2 * levels), :] = total_c[inner:]
    v_scr[...] = total_v

    def some(s, _):
        products = [[] for _ in range(members)]
        for n in range(chunk):
            k = s * chunk + n
            here = pl.multiple_of(k * rows, rows)
            u = u_scr[pl.ds(here, rows), :]
            v = v_scr[pl.ds(here, rows), :]
            for m in range(members):
                products[m].append(u * pert_ref[m, 0, k].astype(F32) + v * pert_ref[m, 1, k].astype(F32))
        high, lower = split(jnp.concatenate([p for one in products for p in one], axis=0))
        got = dot_nn(high, table) + dot_nn(lower, table)
        block = chunk * rows
        for m in range(members):
            to = pl.multiple_of(m * inner + s * block, block)
            f_scr[pl.ds(to, block), :] = got[m * block : (m + 1) * block]
        return 0

    lax.fori_loop(0, levels // chunk, some, 0)

    out = {}

    def add(i, value):
        low, w0, w1 = weights_x(i, ratio)
        for at, w in ((low, w0), (low + 1, w1)):
            out[at] = w * value if at not in out else out[at] + w * value

    for side in range(2):
        u = u_scr[pl.ds(inner + side * levels, levels), :]
        v = v_scr[pl.ds(inner + side * levels, levels), :]
        product = []
        for m in range(members):
            halo = []
            for part in range(2):
                e, o = even_ref[m, part], odd_ref[m, part]
                halo.append(jnp.where(even, o, e) if side == 0 else jnp.where(even, e, o))
            product.append(u * halo[0] + v * halo[1])
        high, lower = split(jnp.concatenate(product, axis=0))
        got = dot_nn(high, table) + dot_nn(lower, table)
        add(-1 if side == 0 else rows, got)
    for i in range(rows):
        add(i, f_scr[pl.ds(i, pairs, stride=rows), :])
    held = {r: mask_row(value * scale, r, coarse_rows, region, regions) for r, value in out.items()}
    for done in range(PASSES):
        reach = 2 + done
        held = {
            r: mask_row(one_pass(held, r, coarse_columns), r, coarse_rows, region, regions)
            for r in range(-reach, coarse_rows + reach)
        }
    for r in range(coarse_rows):
        own_out[r] = held[r]
    for k in range(HALO):
        before, after = held[k - HALO], held[coarse_rows + k]
        a_out[k] = jnp.where(even, after, before)
        b_out[k] = jnp.where(even, before, after)


def backward(q_terms, kind, value, weight, pert, halo_even, halo_odd, hot, scale, coarse_rows, coarse_columns):
    members, _, levels, rows, columns = pert.shape
    pairs = members * levels
    chunk = 2 if levels % 2 == 0 else 1
    outs = [jax.ShapeDtypeStruct((n, pairs, coarse_columns), F32) for n in (coarse_rows, HALO, HALO)]
    return pl.pallas_call(
        functools.partial(backward_kernel, scale, chunk, len(q_terms)),
        out_shape=outs,
        scratch_shapes=[
            pltpu.VMEM((levels * rows + 2 * levels, columns), F32),
            pltpu.VMEM((levels * rows + 2 * levels, columns), F32),
            pltpu.VMEM((pairs * rows, coarse_columns), F32),
        ],
        compiler_params=params(28),
        name="adjoint_to_coarse",
    )(*q_terms, kind, value, weight, pert, halo_even, halo_odd, *hot)


def join_kernel(coarse_rows, own_ref, even_ref, odd_ref, out_ref):
    even = lax.rem(lax.axis_index("reg"), 2) == 0
    pairs = own_ref.shape[1]
    for r in range(coarse_rows):
        total = own_ref[r]
        if r < HALO:
            total = total + jnp.where(even, odd_ref[r], even_ref[r])
        k = r - (coarse_rows - HALO)
        if k >= 0:
            total = total + jnp.where(even, even_ref[k], odd_ref[k])
        out_ref[pl.ds(r, pairs, stride=coarse_rows), :] = total


def join(own, got_even, got_odd):
    coarse_rows, pairs, columns = own.shape
    return pl.pallas_call(
        functools.partial(join_kernel, coarse_rows),
        out_shape=jax.ShapeDtypeStruct((pairs * coarse_rows, columns), F32),
        compiler_params=params(16),
        name="join_rows",
    )(own, got_even, got_odd)


def local(alpha, perturbation, obs_cell, obs_kind, obs_value, obs_weight):
    members, levels, coarse_rows, coarse_columns = alpha.shape
    scale = 1.0 / math.sqrt(members * lax.axis_size("mem"))
    flat = alpha.reshape(-1, coarse_columns)
    cell, kind, value, weight = (x.reshape(1, -1) for x in (obs_cell, obs_kind, obs_value, obs_weight))
    perturbation, pack_a, pack_b, hot, own = prepare(perturbation, cell, kind, flat, coarse_rows)
    flat_odd = swap_odd(flat)
    flat_even = swap_even(flat)
    halo_odd = swap_odd(pack_b)
    halo_even = swap_even(pack_a)
    q, edge_fine = forward(own, flat_even, flat_odd, perturbation, hot, scale)
    q = edge(q, edge_fine, halo_even, halo_odd, hot, members, levels)
    terms = others(q, "mem")
    own, send_a, send_b = backward(
        terms, kind, value, weight, perturbation, halo_even, halo_odd, hot, scale,
        coarse_rows, coarse_columns,
    )
    got_odd = swap_odd(send_b)
    got_even = swap_even(send_a)
    return join(own, got_even, got_odd).reshape(alpha.shape)


def solution(mesh):
    return jax.shard_map(
        local,
        mesh=mesh,
        in_specs=(
            P("mem", None, "reg", None),
            P("mem", None, None, "reg", None),
            P("reg"),
            P("reg"),
            P("reg"),
            P("reg"),
        ),
        out_specs=P("mem", None, "reg", None),
        check_vma=False,
    )
```

```python
import functools
import math

import jax
import jax.numpy as jnp
from jax import lax
from jax.experimental import pallas as pl
from jax.experimental.pallas import tpu as pltpu
from jax.sharding import PartitionSpec as P


PASSES = 2
HALO = PASSES + 1
DIFFUSE = 0.2
CENTRE = round((1.0 - 4.0 * DIFFUSE) / DIFFUSE)
F32 = jnp.float32
BF16 = jnp.bfloat16


def params(mib):
    return pltpu.CompilerParams(vmem_limit_bytes=mib << 20)


def swap_pairs(n, odd):
    pairs = []
    for i in range(1 if odd else 0, n - 1, 2):
        pairs += [(i, i + 1), (i + 1, i)]
    return pairs


def swap_even(value):
    return lax.ppermute(value, "reg", swap_pairs(lax.axis_size("reg"), False))


def swap_odd(value):
    return lax.ppermute(value, "reg", swap_pairs(lax.axis_size("reg"), True))


def others(value, axis):
    n = lax.axis_size(axis)
    stride = 1
    rounds = []
    while stride < n:
        left = n // stride
        radix = 4 if left % 4 == 0 else 2 if left % 2 == 0 else left
        sends = []
        for k in range(1, radix):
            pairs = []
            for i in range(n):
                digit = (i // stride) % radix
                other = digit ^ k if radix in (2, 4) else (digit + k) % radix
                pairs.append((i, i + (other - digit) * stride))
            sends.append(pairs)
        rounds.append(sends)
        stride *= radix
    for number, sends in enumerate(rounds):
        got = [lax.ppermute(value, axis, pairs) for pairs in sends]
        if number == len(rounds) - 1:
            return [value] + got
        for part in got:
            value = value + part
    return [value]


def split(x):
    high = x.astype(BF16)
    return high, (x - high.astype(F32)).astype(BF16)


def dot_nn(a, b):
    return lax.dot_general(a, b, (((1,), (0,)), ((), ())), preferred_element_type=F32)


def dot_nt(a, b):
    return lax.dot_general(a, b, (((1,), (1,)), ((), ())), preferred_element_type=F32)


def iota(shape, dim):
    return lax.broadcasted_iota(jnp.int32, shape, dim)


def table_y(coarse, fine, coarse_dim):
    shape = (coarse, fine) if coarse_dim == 0 else (fine, coarse)
    ratio = fine // coarse
    at = (iota(shape, 1 - coarse_dim).astype(F32) + 0.5) / ratio - 0.5
    return jnp.maximum(0.0, 1.0 - jnp.abs(at - iota(shape, coarse_dim).astype(F32))).astype(BF16)


def weights_x(i, ratio):
    at = (i + 0.5) / ratio - 0.5
    low = math.floor(at)
    return low, 1.0 - (at - low), at - low


def filters(columns):
    row, column = iota((columns, columns), 0), iota((columns, columns), 1)
    near = jnp.abs(row - column)
    once = jnp.where(near == 0, CENTRE, jnp.where(near == 1, 1.0, 0.0)).astype(BF16)
    twice = dot_nn(once, once).astype(BF16)
    once = once + once
    return jnp.concatenate([twice, twice], axis=0), jnp.concatenate([once, once], axis=0)


def smooth(rows, wanted, coarse_rows, region, regions, twice, once):
    pairs = next(iter(rows.values())).shape[0]

    def both(values):
        high, lower = split(jnp.concatenate(values, axis=0))
        return jnp.concatenate([high, lower], axis=1)

    def total(*names):
        found = [rows[n] for n in names if n in rows]
        return functools.reduce(jnp.add, found) if found else None

    mids = [r for r in wanted if r in rows]
    at_mid = dot_nn(both([rows[r] for r in mids]), twice)
    sides = [r for r in wanted if total(r - 1, r + 1) is not None]
    at_side = dot_nn(both([total(r - 1, r + 1) for r in sides]), once)
    out = {}
    for r in wanted:
        terms = []
        if r in mids:
            k = mids.index(r)
            terms.append(at_mid[k * pairs : (k + 1) * pairs])
            around = 2.0
            if r == 0:
                around = jnp.where(region > 0, 2.0, 1.0)
            elif r == coarse_rows - 1:
                around = jnp.where(region < regions - 1, 2.0, 1.0)
            terms.append(around * rows[r])
        if r in sides:
            k = sides.index(r)
            terms.append(at_side[k * pairs : (k + 1) * pairs])
        far = total(r - 2, r + 2)
        if far is not None:
            terms.append(far)
        out[r] = (DIFFUSE * DIFFUSE) * functools.reduce(jnp.add, terms)
    return out


def mask_row(value, index, coarse_rows, region, regions):
    if index < 0:
        return jnp.where(region * coarse_rows + index >= 0, value, 0.0)
    if index >= coarse_rows:
        return jnp.where(region * coarse_rows + index < regions * coarse_rows, value, 0.0)
    return value


def decode(cell, rows, columns):
    plane = rows * columns
    level = cell // plane
    rest = cell - level * plane
    row = rest // columns
    return level, row, rest - row * columns


def weights_kernel(up_ref, down_ref, twice_ref, once_ref):
    coarse = twice_ref.shape[1]
    fine = up_ref.shape[1]
    up = table_y(coarse, fine, 0)
    up_ref[...] = jnp.concatenate([up, up], axis=0)
    down_ref[...] = table_y(coarse, fine, 1)
    twice_ref[...], once_ref[...] = filters(coarse)


def weights(coarse, fine):
    shapes = ((2 * coarse, fine), (fine, coarse), (2 * coarse, coarse), (2 * coarse, coarse))
    return pl.pallas_call(
        weights_kernel,
        out_shape=[jax.ShapeDtypeStruct(shape, BF16) for shape in shapes],
        compiler_params=params(16),
        cost_estimate=pl.CostEstimate(flops=1 << 33, bytes_accessed=1 << 24, transcendentals=0),
        name="weights",
    )()


def pack_kernel(
    pert_ref, cell_hbm, kind_hbm, flat_hbm,
    a_ref, b_ref, cell_ref, kind_ref, own_ref,
    flat_ref, sem,
):
    members, parts, levels, rows, columns = pert_ref.shape
    copies = []
    for n, (source, to) in enumerate(((cell_hbm, cell_ref), (kind_hbm, kind_ref), (flat_hbm, flat_ref))):
        copy = pltpu.make_async_copy(source, to, sem.at[n])
        copy.start()
        copies.append(copy)
    inner = levels * rows
    even = lax.rem(lax.axis_index("reg"), 2) == 0
    shape = (2 * levels, inner)
    pick = iota(shape, 0)
    to_a = pick < levels
    edge = jnp.where(to_a == even, rows - 1, 0)
    wanted = jnp.where(to_a, pick, pick - levels) * rows + edge
    chooser = jnp.where(iota(shape, 1) == wanted, 1.0, 0.0).astype(BF16)
    for m in range(members):
        for part in range(parts):
            got = dot_nn(chooser, pert_ref[m, part].reshape(inner, columns))
            a_ref[m, part] = got[:levels]
            b_ref[m, part] = got[levels:]
    for copy in copies:
        copy.wait()
    coarse_rows, pairs, _ = own_ref.shape
    for r in range(coarse_rows):
        own_ref[r] = flat_ref[pl.ds(r, pairs, stride=coarse_rows), :]


def pack(pert, cell, kind, flat, coarse_rows):
    members, parts, levels, _, columns = pert.shape
    shapes = [jax.ShapeDtypeStruct((members, parts, levels, columns), F32)] * 2
    shapes += [jax.ShapeDtypeStruct(cell.shape, cell.dtype)] * 2
    shapes.append(jax.ShapeDtypeStruct((coarse_rows, flat.shape[0] // coarse_rows, flat.shape[1]), F32))
    vmem = pl.BlockSpec(memory_space=pltpu.VMEM)
    hbm = pl.BlockSpec(memory_space=pltpu.HBM)
    cell, kind, flat = (pltpu.with_memory_space_constraint(x, pltpu.HBM) for x in (cell, kind, flat))
    return pl.pallas_call(
        pack_kernel,
        in_specs=[vmem, hbm, hbm, hbm],
        out_specs=[vmem] * len(shapes),
        out_shape=shapes,
        scratch_shapes=[pltpu.VMEM(flat.shape, flat.dtype), pltpu.SemaphoreType.DMA((3,))],
        compiler_params=params(16),
        name="pack_rows",
    )(pert, cell, kind, flat)


def tables_kernel(levels, rows, columns, cell_ref, kind_ref, r0_ref, ru_ref, rv_ref, c0_ref, cy_ref):
    cell, kind = cell_ref[...], kind_ref[...]
    level, row, column = decode(cell, rows, columns)
    line = level * rows + row
    count = cell.shape[1]
    inner = levels * rows
    minus = jnp.where(row > 0, line - 1, inner + level)
    plus = jnp.where(row < rows - 1, line + 1, inner + levels + level)
    none = jnp.full_like(line, -1)
    minus_u = jnp.where(kind == 3, minus, none)
    plus_u = jnp.where(kind == 3, plus, none)
    here_v = jnp.where((kind == 1) | (kind == 3), line, none)
    minus_v = jnp.where(kind == 2, minus, none)
    plus_v = jnp.where(kind == 2, plus, none)
    step = 32

    def lines(k, _):
        start = pl.multiple_of(k * step, step)
        at = iota((step, count), 0) + start
        ru = jnp.where(at == plus_u, 0.5, jnp.where(at == minus_u, -0.5, 0.0))
        rv = jnp.where(at == plus_v, 0.5, jnp.where(at == minus_v, -0.5, jnp.where(at == here_v, 1.0, 0.0)))
        r0 = jnp.where(at == line, 1.0, 0.0)
        ru_ref[pl.ds(start, step), :] = ru.astype(BF16)
        rv_ref[pl.ds(start, step), :] = rv.astype(BF16)
        r0_ref[pl.ds(start, step), :] = r0.astype(BF16)
        return 0

    lax.fori_loop(0, (inner + 2 * levels) // step, lines, 0)

    def cells(k, _):
        start = pl.multiple_of(k * step, step)
        at = iota((step, count), 0) + start
        c0_ref[pl.ds(start, step), :] = jnp.where(at == column, 1.0, 0.0).astype(BF16)
        cy = jnp.where(at == column + 1, 0.5, jnp.where(at == column - 1, -0.5, 0.0))
        cy_ref[pl.ds(start, step), :] = cy.astype(BF16)
        return 0

    lax.fori_loop(0, columns // step, cells, 0)


def tables(cell, kind, levels, rows, columns):
    count = cell.shape[1]
    lines = levels * rows + 2 * levels
    return pl.pallas_call(
        functools.partial(tables_kernel, levels, rows, columns),
        out_shape=[jax.ShapeDtypeStruct((n, count), BF16) for n in (lines, lines, lines, columns, columns)],
        compiler_params=params(16),
        name="one_hots",
    )(cell, kind)


def forward_kernel(
    scale, chunk,
    own_ref, even_ref, odd_ref, up_ref, twice_ref, once_ref, pert_ref, r0_ref, ru_ref, rv_ref, c0_ref, cy_ref,
    q_ref, edge_ref,
    fine_in, fine_scr, t_scr,
):
    region = lax.axis_index("reg")
    regions = lax.axis_size("reg")
    members, _, levels, rows, _ = pert_ref.shape
    coarse_rows, pairs, _ = own_ref.shape
    ratio = rows // coarse_rows
    block = chunk * rows
    inner = levels * rows
    even = lax.rem(region, 2) == 0
    table = up_ref[...]
    rows_in = {r: own_ref[r] for r in range(coarse_rows)}
    for k in range(HALO):
        low = coarse_rows - HALO + k
        e = even_ref[pl.ds(low, pairs, stride=coarse_rows), :]
        o = odd_ref[pl.ds(low, pairs, stride=coarse_rows), :]
        rows_in[k - HALO] = jnp.where(even, o, e)
        e = even_ref[pl.ds(k, pairs, stride=coarse_rows), :]
        o = odd_ref[pl.ds(k, pairs, stride=coarse_rows), :]
        rows_in[coarse_rows + k] = jnp.where(even, e, o)
    rows_in = smooth(
        rows_in, range(-1, coarse_rows + 1), coarse_rows, region, regions, twice_ref[...], once_ref[...]
    )
    rows_in = {r: mask_row(value, r, coarse_rows, region, regions) for r, value in rows_in.items()}
    for i in range(-1, rows + 1):
        low, w0, w1 = weights_x(i, ratio)
        value = (w0 * rows_in[low] + w1 * rows_in[low + 1]) * scale
        if 0 <= i < rows:
            fine_in[pl.ds(i, pairs, stride=rows), :] = value
        else:
            high, lower = split(value)
            got = dot_nn(jnp.concatenate([high, lower], axis=1), table)
            edge_ref[0 if i < 0 else 1] = got

    for step in range(levels // chunk):
        parts = []
        for m in range(members):
            parts.append(fine_in[pl.ds(m * inner + step * block, block), :])
        high, lower = split(jnp.concatenate(parts, axis=0))
        fine_scr[step % 2] = dot_nn(jnp.concatenate([high, lower], axis=1), table)
        for k in range(chunk):
            u = v = None
            for m in range(members):
                fine = fine_scr[step % 2, pl.ds(m * block + k * rows, rows), :]
                pu = fine * pert_ref[m, 0, step * chunk + k].astype(F32)
                pv = fine * pert_ref[m, 1, step * chunk + k].astype(F32)
                u = pu if u is None else u + pu
                v = pv if v is None else v + pv
            for n, value in enumerate((*split(u), *split(v))):
                t_scr[pl.ds(n * inner + step * block + k * rows, rows), :] = value

    count = r0_ref.shape[1]
    width = min(256, count)
    for k in range(count // width):
        at = pl.ds(k * width, width)
        z = dot_nn(t_scr[...], c0_ref[:, at])
        zy = dot_nn(t_scr[pl.ds(0, 2 * inner), :], cy_ref[:, at])
        zu = z[:inner] + z[inner : 2 * inner]
        zv = z[2 * inner : 3 * inner] + z[3 * inner :]
        zy = zy[:inner] + zy[inner:]
        inside = pl.ds(0, inner)
        r0 = r0_ref[inside, at].astype(F32)
        q_ref[pl.ds(0, 1), at] = jnp.sum(r0 * zu, axis=0, keepdims=True)
        q_ref[pl.ds(1, 1), at] = jnp.sum(rv_ref[inside, at].astype(F32) * zv, axis=0, keepdims=True)
        q_ref[pl.ds(2, 1), at] = jnp.sum(ru_ref[inside, at].astype(F32) * zu, axis=0, keepdims=True)
        q_ref[pl.ds(3, 1), at] = jnp.sum(r0 * zy, axis=0, keepdims=True)


def forward(own, got_even, got_odd, weight, pert, hot, scale):
    up, _, twice, once = weight
    members, _, levels, rows, columns = pert.shape
    _, pairs, coarse_columns = own.shape
    chunk = 4 if levels % 4 == 0 else 1
    count = hot[0].shape[1]
    return pl.pallas_call(
        functools.partial(forward_kernel, scale, chunk),
        out_shape=[jax.ShapeDtypeStruct((4, count), F32),
                   jax.ShapeDtypeStruct((2, pairs, columns), F32)],
        scratch_shapes=[
            pltpu.VMEM((pairs * rows, coarse_columns), F32),
            pltpu.VMEM((2, members * chunk * rows, columns), F32),
            pltpu.VMEM((4 * levels * rows, columns), BF16),
        ],
        compiler_params=params(28),
        name="increment_at_obs",
    )(own, got_even, got_odd, up, twice, once, pert, *hot)


def edge_kernel(members, levels, q_ref, fine_ref, even_ref, odd_ref, ru_ref, rv_ref, c0_ref, out_ref):
    even = lax.rem(lax.axis_index("reg"), 2) == 0
    table = []
    for part in range(2):
        for side in range(2):
            total = None
            for m in range(members):
                e, o = even_ref[m, part], odd_ref[m, part]
                halo = jnp.where(even, o, e) if side == 0 else jnp.where(even, e, o)
                term = fine_ref[side, pl.ds(m * levels, levels), :] * halo
                total = term if total is None else total + term
            table.append(total)
    high, lower = split(jnp.concatenate(table, axis=0))
    z = dot_nn(jnp.concatenate([high, lower], axis=0), c0_ref[...])
    tail = 2 * levels
    z = z[: 2 * tail] + z[2 * tail :]
    rim = pl.ds(ru_ref.shape[0] - tail, tail)
    in_u = jnp.sum(ru_ref[rim, :].astype(F32) * z[:tail], axis=0, keepdims=True)
    in_v = jnp.sum(rv_ref[rim, :].astype(F32) * z[tail:], axis=0, keepdims=True)
    out_ref[pl.ds(0, 1), :] = q_ref[pl.ds(0, 1), :]
    out_ref[pl.ds(1, 1), :] = q_ref[pl.ds(1, 1), :] + in_v
    out_ref[pl.ds(2, 1), :] = q_ref[pl.ds(2, 1), :] + in_u
    out_ref[pl.ds(3, 1), :] = q_ref[pl.ds(3, 1), :]


def edge(q, fine, halo_even, halo_odd, hot, members, levels):
    _, ru, rv, c0, _ = hot
    return pl.pallas_call(
        functools.partial(edge_kernel, members, levels),
        out_shape=jax.ShapeDtypeStruct(q.shape, F32),
        compiler_params=params(16),
        name="edge_at_obs",
    )(q, fine, halo_even, halo_odd, ru, rv, c0)


def backward_kernel(scale, chunk, terms, *refs):
    q_refs = refs[:terms]
    (kind_ref, value_ref, weight_ref, down_ref, twice_ref, once_ref, pert_ref, even_ref, odd_ref,
     r0_ref, ru_ref, rv_ref, c0_ref, cy_ref,
     own_out, a_out, b_out,
     u_scr, v_scr, f_scr) = refs[terms:]
    region = lax.axis_index("reg")
    regions = lax.axis_size("reg")
    members, _, levels, rows, _ = pert_ref.shape
    coarse_rows, pairs, _ = own_out.shape
    ratio = rows // coarse_rows
    inner = levels * rows
    even = lax.rem(region, 2) == 0
    table = down_ref[...]

    q = q_refs[0][...]
    for ref in q_refs[1:]:
        q = q + ref[...]
    q0, q1, q2, q3 = (q[n : n + 1] for n in range(4))
    kind = kind_ref[...]
    seen = jnp.where(kind == 0, q0, jnp.where(kind == 1, q1, jnp.where(kind == 2, q1 - q3, q0 * q2 + q1 * q3)))
    misfit = weight_ref[...] * (seen - value_ref[...])
    zero = jnp.zeros_like(misfit)
    a = jnp.where(kind == 0, misfit, jnp.where(kind == 3, misfit * q2, zero))
    b = jnp.where(kind == 2, -misfit, jnp.where(kind == 3, misfit * q1, zero))
    c = jnp.where(kind == 3, misfit * q0, zero)
    g = jnp.where(kind == 3, misfit * q3, jnp.where(kind == 0, zero, misfit))
    r0, ru, rv = r0_ref[...], ru_ref[...], rv_ref[...]
    lines = r0.shape[0]
    left = [r0 * x + ru * y for x, y in zip(split(a), split(c))] + [rv * x for x in split(g)]
    both = dot_nt(jnp.concatenate(left, axis=0), c0_ref[...])
    left = [r0[:inner] * x for x in split(b)]
    along = dot_nt(jnp.concatenate(left, axis=0), cy_ref[...])
    total = both[:lines] + both[lines : 2 * lines]
    u_scr[pl.ds(0, inner), :] = total[:inner] + (along[:inner] + along[inner:])
    u_scr[pl.ds(inner, lines - inner), :] = total[inner:]
    v_scr[...] = both[2 * lines : 3 * lines] + both[3 * lines :]

    block = chunk * rows
    for s in range(levels // chunk):
        product = []
        for m in range(members):
            for n in range(chunk):
                k = s * chunk + n
                u = u_scr[pl.ds(k * rows, rows), :]
                v = v_scr[pl.ds(k * rows, rows), :]
                product.append(u * pert_ref[m, 0, k].astype(F32) + v * pert_ref[m, 1, k].astype(F32))
        high, lower = split(jnp.concatenate(product, axis=0))
        got = dot_nn(high, table) + dot_nn(lower, table)
        for m in range(members):
            f_scr[pl.ds(m * inner + s * block, block), :] = got[m * block : (m + 1) * block]

    out = {}

    def add(i, value):
        low, w0, w1 = weights_x(i, ratio)
        for at, w in ((low, w0), (low + 1, w1)):
            out[at] = w * value if at not in out else out[at] + w * value

    for side in range(2):
        u = u_scr[pl.ds(inner + side * levels, levels), :]
        v = v_scr[pl.ds(inner + side * levels, levels), :]
        product = []
        for m in range(members):
            halo = []
            for part in range(2):
                e, o = even_ref[m, part], odd_ref[m, part]
                halo.append(jnp.where(even, o, e) if side == 0 else jnp.where(even, e, o))
            product.append(u * halo[0] + v * halo[1])
        high, lower = split(jnp.concatenate(product, axis=0))
        got = dot_nn(high, table) + dot_nn(lower, table)
        add(-1 if side == 0 else rows, got)
    for i in range(rows):
        add(i, f_scr[pl.ds(i, pairs, stride=rows), :])
    held = {r: mask_row(value * scale, r, coarse_rows, region, regions) for r, value in out.items()}
    held = smooth(
        held, range(-HALO, coarse_rows + HALO), coarse_rows, region, regions, twice_ref[...], once_ref[...]
    )
    for r in range(coarse_rows):
        own_out[r] = held[r]
    for k in range(HALO):
        before, after = held[k - HALO], held[coarse_rows + k]
        a_out[k] = jnp.where(even, after, before)
        b_out[k] = jnp.where(even, before, after)


def backward(q_terms, kind, value, weight, tables_y, pert, halo_even, halo_odd, hot, scale, coarse_rows, coarse_columns):
    members, _, levels, rows, columns = pert.shape
    pairs = members * levels
    chunk = 4 if levels % 4 == 0 else 1
    outs = [jax.ShapeDtypeStruct((n, pairs, coarse_columns), F32) for n in (coarse_rows, HALO, HALO)]
    return pl.pallas_call(
        functools.partial(backward_kernel, scale, chunk, len(q_terms)),
        out_shape=outs,
        scratch_shapes=[
            pltpu.VMEM((levels * rows + 2 * levels, columns), F32),
            pltpu.VMEM((levels * rows + 2 * levels, columns), F32),
            pltpu.VMEM((pairs * rows, coarse_columns), F32),
        ],
        compiler_params=params(28),
        name="adjoint_to_coarse",
    )(*q_terms, kind, value, weight, *tables_y[1:], pert, halo_even, halo_odd, *hot)


def join_kernel(coarse_rows, own_ref, even_ref, odd_ref, out_ref):
    even = lax.rem(lax.axis_index("reg"), 2) == 0
    pairs = own_ref.shape[1]
    for r in range(coarse_rows):
        total = own_ref[r]
        if r < HALO:
            total = total + jnp.where(even, odd_ref[r], even_ref[r])
        k = r - (coarse_rows - HALO)
        if k >= 0:
            total = total + jnp.where(even, even_ref[k], odd_ref[k])
        out_ref[pl.ds(r, pairs, stride=coarse_rows), :] = total


def join(own, got_even, got_odd):
    coarse_rows, pairs, columns = own.shape
    return pl.pallas_call(
        functools.partial(join_kernel, coarse_rows),
        out_shape=jax.ShapeDtypeStruct((pairs * coarse_rows, columns), F32),
        compiler_params=params(16),
        name="join_rows",
    )(own, got_even, got_odd)


def local(alpha, perturbation, obs_cell, obs_kind, obs_value, obs_weight):
    members, levels, coarse_rows, coarse_columns = alpha.shape
    _, _, _, rows, columns = perturbation.shape
    scale = 1.0 / math.sqrt(members * lax.axis_size("mem"))
    flat = alpha.reshape(-1, coarse_columns)
    cell, kind, value, weight = (x.reshape(1, -1) for x in (obs_cell, obs_kind, obs_value, obs_weight))
    along_y = weights(coarse_columns, columns)
    flat_odd = swap_odd(flat)
    flat_even = swap_even(flat)
    pack_a, pack_b, cell, kind, own = pack(perturbation, cell, kind, flat, coarse_rows)
    halo_odd = swap_odd(pack_b)
    halo_even = swap_even(pack_a)
    hot = tables(cell, kind, levels, rows, columns)
    q, edge_fine = forward(own, flat_even, flat_odd, along_y, perturbation, hot, scale)
    q = edge(q, edge_fine, halo_even, halo_odd, hot, members, levels)
    terms = others(q, "mem")
    own, send_a, send_b = backward(
        terms, kind, value, weight, along_y, perturbation, halo_even, halo_odd, hot, scale,
        coarse_rows, coarse_columns,
    )
    got_odd = swap_odd(send_b)
    got_even = swap_even(send_a)
    return join(own, got_even, got_odd).reshape(alpha.shape)


def solution(mesh):
    return jax.shard_map(
        local,
        mesh=mesh,
        in_specs=(
            P("mem", None, "reg", None),
            P("mem", None, None, "reg", None),
            P("reg"),
            P("reg"),
            P("reg"),
            P("reg"),
        ),
        out_specs=P("mem", None, "reg", None),
        check_vma=False,
    )
```

```python
import functools
import math

import jax
import jax.numpy as jnp
from jax import lax
from jax.experimental import pallas as pl
from jax.experimental.pallas import tpu as pltpu
from jax.sharding import PartitionSpec as P


PASSES = 2
HALO = PASSES + 1
DIFFUSE = 0.2
CENTRE = round((1.0 - 4.0 * DIFFUSE) / DIFFUSE)
F32 = jnp.float32
BF16 = jnp.bfloat16


def params(mib):
    return pltpu.CompilerParams(vmem_limit_bytes=mib << 20)


def swap_pairs(n, odd):
    pairs = []
    for i in range(1 if odd else 0, n - 1, 2):
        pairs += [(i, i + 1), (i + 1, i)]
    return pairs


def swap_even(value):
    return lax.ppermute(value, "reg", swap_pairs(lax.axis_size("reg"), False))


def swap_odd(value):
    return lax.ppermute(value, "reg", swap_pairs(lax.axis_size("reg"), True))


def others(value, axis):
    n = lax.axis_size(axis)
    stride = 1
    rounds = []
    while stride < n:
        left = n // stride
        radix = 4 if left % 4 == 0 else 2 if left % 2 == 0 else left
        sends = []
        for k in range(1, radix):
            pairs = []
            for i in range(n):
                digit = (i // stride) % radix
                other = digit ^ k if radix in (2, 4) else (digit + k) % radix
                pairs.append((i, i + (other - digit) * stride))
            sends.append(pairs)
        rounds.append(sends)
        stride *= radix
    for number, sends in enumerate(rounds):
        got = []
        for pairs in sends:
            got.append(lax.ppermute(value, axis, pairs))
        if number == len(rounds) - 1:
            return [value] + got
        for part in got:
            value = value + part
    return [value]


def split(x):
    high = x.astype(BF16)
    return high, (x - high.astype(F32)).astype(BF16)


def dot_nn(a, b):
    return lax.dot_general(a, b, (((1,), (0,)), ((), ())), preferred_element_type=F32)


def dot_nt(a, b):
    return lax.dot_general(a, b, (((1,), (1,)), ((), ())), preferred_element_type=F32)


def iota(shape, dim):
    return lax.broadcasted_iota(jnp.int32, shape, dim)


def table_y(coarse, fine, coarse_dim):
    shape = (coarse, fine) if coarse_dim == 0 else (fine, coarse)
    ratio = fine // coarse
    at = (iota(shape, 1 - coarse_dim).astype(F32) + 0.5) / ratio - 0.5
    return jnp.maximum(0.0, 1.0 - jnp.abs(at - iota(shape, coarse_dim).astype(F32))).astype(BF16)


def weights_x(i, ratio):
    at = (i + 0.5) / ratio - 0.5
    low = math.floor(at)
    return low, 1.0 - (at - low), at - low


def filters(columns):
    row, column = iota((columns, columns), 0), iota((columns, columns), 1)
    near = jnp.abs(row - column)
    once = jnp.where(near == 0, CENTRE, jnp.where(near == 1, 1.0, 0.0)).astype(BF16)
    twice = dot_nn(once, once).astype(BF16)
    once = once + once
    return jnp.concatenate([twice, twice], axis=0), jnp.concatenate([once, once], axis=0)


def smooth(rows, wanted, coarse_rows, region, regions, twice, once):
    pairs = next(iter(rows.values())).shape[0]

    def both(values):
        high, lower = split(jnp.concatenate(values, axis=0))
        return jnp.concatenate([high, lower], axis=1)

    def total(*names):
        found = [rows[n] for n in names if n in rows]
        return functools.reduce(jnp.add, found) if found else None

    mids = [r for r in wanted if r in rows]
    at_mid = dot_nn(both([rows[r] for r in mids]), twice)
    sides = [r for r in wanted if total(r - 1, r + 1) is not None]
    at_side = dot_nn(both([total(r - 1, r + 1) for r in sides]), once)
    out = {}
    for r in wanted:
        terms = []
        if r in mids:
            k = mids.index(r)
            terms.append(at_mid[k * pairs : (k + 1) * pairs])
            around = 2.0
            if r == 0:
                around = jnp.where(region > 0, 2.0, 1.0)
            elif r == coarse_rows - 1:
                around = jnp.where(region < regions - 1, 2.0, 1.0)
            terms.append(around * rows[r])
        if r in sides:
            k = sides.index(r)
            terms.append(at_side[k * pairs : (k + 1) * pairs])
        far = total(r - 2, r + 2)
        if far is not None:
            terms.append(far)
        out[r] = (DIFFUSE * DIFFUSE) * functools.reduce(jnp.add, terms)
    return out


def mask_row(value, index, coarse_rows, region, regions):
    if index < 0:
        return jnp.where(region * coarse_rows + index >= 0, value, 0.0)
    if index >= coarse_rows:
        return jnp.where(region * coarse_rows + index < regions * coarse_rows, value, 0.0)
    return value


def decode(cell, rows, columns):
    plane = rows * columns
    level = cell // plane
    rest = cell - level * plane
    row = rest // columns
    return level, row, rest - row * columns


def down_kernel(down_ref):
    fine, coarse = down_ref.shape
    down_ref[...] = table_y(coarse, fine, 1)


def down_weights(coarse, fine):
    return pl.pallas_call(
        down_kernel,
        out_shape=jax.ShapeDtypeStruct((fine, coarse), BF16),
        compiler_params=params(16),
        cost_estimate=pl.CostEstimate(flops=1160000000, bytes_accessed=1 << 20, transcendentals=0),
        name="down_weights",
    )()


def pack_kernel(pert_ref, a_ref, b_ref):
    members, parts, levels, rows, columns = pert_ref.shape
    inner = levels * rows
    even = lax.rem(lax.axis_index("reg"), 2) == 0
    shape = (2 * levels, inner)
    pick = iota(shape, 0)
    to_a = pick < levels
    edge = jnp.where(to_a == even, rows - 1, 0)
    wanted = jnp.where(to_a, pick, pick - levels) * rows + edge
    chooser = jnp.where(iota(shape, 1) == wanted, 1.0, 0.0).astype(BF16)
    for m in range(members):
        for part in range(parts):
            got = dot_nn(chooser, pert_ref[m, part].reshape(inner, columns))
            a_ref[m, part] = got[:levels]
            b_ref[m, part] = got[levels:]


def pack(pert):
    members, parts, levels, _, columns = pert.shape
    out = jax.ShapeDtypeStruct((members, parts, levels, columns), F32)
    return pl.pallas_call(
        pack_kernel,
        out_shape=[out, out],
        compiler_params=params(16),
        name="pack_rows",
    )(pert)


def tables_kernel(
    levels, rows, columns, cell_ref, kind_ref, r0_ref, ru_ref, rv_ref, c0_ref, cy_ref, up_ref, twice_ref, once_ref
):
    coarse = twice_ref.shape[1]
    up = table_y(coarse, columns, 0)
    up_ref[...] = jnp.concatenate([up, up], axis=0)
    twice_ref[...], once_ref[...] = filters(coarse)
    cell, kind = cell_ref[...], kind_ref[...]
    level, row, column = decode(cell, rows, columns)
    line = level * rows + row
    count = cell.shape[1]
    inner = levels * rows
    minus = jnp.where(row > 0, line - 1, inner + level)
    plus = jnp.where(row < rows - 1, line + 1, inner + levels + level)
    none = jnp.full_like(line, -1)
    minus_u = jnp.where(kind == 3, minus, none)
    plus_u = jnp.where(kind == 3, plus, none)
    here_v = jnp.where((kind == 1) | (kind == 3), line, none)
    minus_v = jnp.where(kind == 2, minus, none)
    plus_v = jnp.where(kind == 2, plus, none)
    step = 32

    def lines(k, _):
        start = pl.multiple_of(k * step, step)
        at = iota((step, count), 0) + start
        ru = jnp.where(at == plus_u, 0.5, jnp.where(at == minus_u, -0.5, 0.0))
        rv = jnp.where(at == plus_v, 0.5, jnp.where(at == minus_v, -0.5, jnp.where(at == here_v, 1.0, 0.0)))
        r0 = jnp.where(at == line, 1.0, 0.0)
        ru_ref[pl.ds(start, step), :] = ru.astype(BF16)
        rv_ref[pl.ds(start, step), :] = rv.astype(BF16)
        r0_ref[pl.ds(start, step), :] = r0.astype(BF16)
        return 0

    lax.fori_loop(0, (inner + 2 * levels) // step, lines, 0)

    def cells(k, _):
        start = pl.multiple_of(k * step, step)
        at = iota((step, count), 0) + start
        c0_ref[pl.ds(start, step), :] = jnp.where(at == column, 1.0, 0.0).astype(BF16)
        cy = jnp.where(at == column + 1, 0.5, jnp.where(at == column - 1, -0.5, 0.0))
        cy_ref[pl.ds(start, step), :] = cy.astype(BF16)
        return 0

    lax.fori_loop(0, columns // step, cells, 0)


def tables(cell, kind, levels, rows, columns, coarse):
    count = cell.shape[1]
    lines = levels * rows + 2 * levels
    shapes = [(n, count) for n in (lines, lines, lines, columns, columns)]
    shapes += [(2 * coarse, columns), (2 * coarse, coarse), (2 * coarse, coarse)]
    made = pl.pallas_call(
        functools.partial(tables_kernel, levels, rows, columns),
        out_shape=[jax.ShapeDtypeStruct(shape, BF16) for shape in shapes],
        compiler_params=params(16),
        name="one_hots",
    )(cell, kind)
    return made[:5], made[5:]


def forward_kernel(
    scale, chunk,
    own_ref, even_ref, odd_ref, up_ref, twice_ref, once_ref, pert_ref, r0_ref, ru_ref, rv_ref, c0_ref, cy_ref,
    q_ref, edge_ref,
    fine_in, fine_scr, t_scr,
):
    region = lax.axis_index("reg")
    regions = lax.axis_size("reg")
    members, _, levels, rows, _ = pert_ref.shape
    pairs = members * levels
    coarse_rows = own_ref.shape[0] // pairs
    ratio = rows // coarse_rows
    block = chunk * rows
    inner = levels * rows
    even = lax.rem(region, 2) == 0
    table = up_ref[...]
    rows_in = {r: own_ref[pl.ds(r, pairs, stride=coarse_rows), :] for r in range(coarse_rows)}
    for k in range(HALO):
        low = coarse_rows - HALO + k
        e = even_ref[pl.ds(low, pairs, stride=coarse_rows), :]
        o = odd_ref[pl.ds(low, pairs, stride=coarse_rows), :]
        rows_in[k - HALO] = jnp.where(even, o, e)
        e = even_ref[pl.ds(k, pairs, stride=coarse_rows), :]
        o = odd_ref[pl.ds(k, pairs, stride=coarse_rows), :]
        rows_in[coarse_rows + k] = jnp.where(even, e, o)
    rows_in = smooth(
        rows_in, range(-1, coarse_rows + 1), coarse_rows, region, regions, twice_ref[...], once_ref[...]
    )
    rows_in = {r: mask_row(value, r, coarse_rows, region, regions) for r, value in rows_in.items()}
    for i in range(-1, rows + 1):
        low, w0, w1 = weights_x(i, ratio)
        value = (w0 * rows_in[low] + w1 * rows_in[low + 1]) * scale
        if 0 <= i < rows:
            fine_in[pl.ds(i, pairs, stride=rows), :] = value
        else:
            high, lower = split(value)
            got = dot_nn(jnp.concatenate([high, lower], axis=1), table)
            edge_ref[0 if i < 0 else 1] = got

    for step in range(levels // chunk):
        parts = []
        for m in range(members):
            parts.append(fine_in[pl.ds(m * inner + step * block, block), :])
        high, lower = split(jnp.concatenate(parts, axis=0))
        fine_scr[step % 2] = dot_nn(jnp.concatenate([high, lower], axis=1), table)
        for k in range(chunk):
            u = v = None
            for m in range(members):
                fine = fine_scr[step % 2, pl.ds(m * block + k * rows, rows), :]
                pu = fine * pert_ref[m, 0, step * chunk + k].astype(F32)
                pv = fine * pert_ref[m, 1, step * chunk + k].astype(F32)
                u = pu if u is None else u + pu
                v = pv if v is None else v + pv
            for n, value in enumerate((*split(u), *split(v))):
                t_scr[pl.ds(n * inner + step * block + k * rows, rows), :] = value

    count = r0_ref.shape[1]
    width = min(256, count)
    for k in range(count // width):
        at = pl.ds(k * width, width)
        z = dot_nn(t_scr[...], c0_ref[:, at])
        zy = dot_nn(t_scr[pl.ds(0, 2 * inner), :], cy_ref[:, at])
        zu = z[:inner] + z[inner : 2 * inner]
        zv = z[2 * inner : 3 * inner] + z[3 * inner :]
        zy = zy[:inner] + zy[inner:]
        inside = pl.ds(0, inner)
        r0 = r0_ref[inside, at].astype(F32)
        q_ref[pl.ds(0, 1), at] = jnp.sum(r0 * zu, axis=0, keepdims=True)
        q_ref[pl.ds(1, 1), at] = jnp.sum(rv_ref[inside, at].astype(F32) * zv, axis=0, keepdims=True)
        q_ref[pl.ds(2, 1), at] = jnp.sum(ru_ref[inside, at].astype(F32) * zu, axis=0, keepdims=True)
        q_ref[pl.ds(3, 1), at] = jnp.sum(r0 * zy, axis=0, keepdims=True)


def forward(own, got_even, got_odd, weight, pert, hot, scale):
    up, twice, once = weight
    members, _, levels, rows, columns = pert.shape
    pairs, coarse_columns = members * levels, own.shape[1]
    chunk = 4 if levels % 4 == 0 else 1
    count = hot[0].shape[1]
    return pl.pallas_call(
        functools.partial(forward_kernel, scale, chunk),
        out_shape=[jax.ShapeDtypeStruct((4, count), F32),
                   jax.ShapeDtypeStruct((2, pairs, columns), F32)],
        scratch_shapes=[
            pltpu.VMEM((pairs * rows, coarse_columns), F32),
            pltpu.VMEM((2, members * chunk * rows, columns), F32),
            pltpu.VMEM((4 * levels * rows, columns), BF16),
        ],
        compiler_params=params(28),
        name="increment_at_obs",
    )(own, got_even, got_odd, up, twice, once, pert, *hot)


def edge_kernel(members, levels, q_ref, fine_ref, even_ref, odd_ref, ru_ref, rv_ref, c0_ref, out_ref):
    even = lax.rem(lax.axis_index("reg"), 2) == 0
    table = []
    for part in range(2):
        for side in range(2):
            total = None
            for m in range(members):
                e, o = even_ref[m, part], odd_ref[m, part]
                halo = jnp.where(even, o, e) if side == 0 else jnp.where(even, e, o)
                term = fine_ref[side, pl.ds(m * levels, levels), :] * halo
                total = term if total is None else total + term
            table.append(total)
    high, lower = split(jnp.concatenate(table, axis=0))
    z = dot_nn(jnp.concatenate([high, lower], axis=0), c0_ref[...])
    tail = 2 * levels
    z = z[: 2 * tail] + z[2 * tail :]
    rim = pl.ds(ru_ref.shape[0] - tail, tail)
    in_u = jnp.sum(ru_ref[rim, :].astype(F32) * z[:tail], axis=0, keepdims=True)
    in_v = jnp.sum(rv_ref[rim, :].astype(F32) * z[tail:], axis=0, keepdims=True)
    out_ref[pl.ds(0, 1), :] = q_ref[pl.ds(0, 1), :]
    out_ref[pl.ds(1, 1), :] = q_ref[pl.ds(1, 1), :] + in_v
    out_ref[pl.ds(2, 1), :] = q_ref[pl.ds(2, 1), :] + in_u
    out_ref[pl.ds(3, 1), :] = q_ref[pl.ds(3, 1), :]


def edge(q, fine, halo_even, halo_odd, hot, members, levels):
    _, ru, rv, c0, _ = hot
    return pl.pallas_call(
        functools.partial(edge_kernel, members, levels),
        out_shape=jax.ShapeDtypeStruct(q.shape, F32),
        compiler_params=params(16),
        name="edge_at_obs",
    )(q, fine, halo_even, halo_odd, ru, rv, c0)


def backward_kernel(scale, chunk, terms, *refs):
    q_refs = refs[:terms]
    (kind_ref, value_ref, weight_ref, down_ref, twice_ref, once_ref, pert_ref, even_ref, odd_ref,
     r0_ref, ru_ref, rv_ref, c0_ref, cy_ref,
     own_out, a_out, b_out,
     u_scr, v_scr, f_scr) = refs[terms:]
    region = lax.axis_index("reg")
    regions = lax.axis_size("reg")
    members, _, levels, rows, _ = pert_ref.shape
    coarse_rows, pairs, _ = own_out.shape
    ratio = rows // coarse_rows
    inner = levels * rows
    even = lax.rem(region, 2) == 0
    table = down_ref[...]

    q = q_refs[0][...]
    for ref in q_refs[1:]:
        q = q + ref[...]
    q0, q1, q2, q3 = (q[n : n + 1] for n in range(4))
    kind = kind_ref[...]
    seen = jnp.where(kind == 0, q0, jnp.where(kind == 1, q1, jnp.where(kind == 2, q1 - q3, q0 * q2 + q1 * q3)))
    misfit = weight_ref[...] * (seen - value_ref[...])
    zero = jnp.zeros_like(misfit)
    a = jnp.where(kind == 0, misfit, jnp.where(kind == 3, misfit * q2, zero))
    b = jnp.where(kind == 2, -misfit, jnp.where(kind == 3, misfit * q1, zero))
    c = jnp.where(kind == 3, misfit * q0, zero)
    g = jnp.where(kind == 3, misfit * q3, jnp.where(kind == 0, zero, misfit))
    r0, ru, rv = r0_ref[...], ru_ref[...], rv_ref[...]
    lines = r0.shape[0]
    left = [r0 * x + ru * y for x, y in zip(split(a), split(c))] + [rv * x for x in split(g)]
    both = dot_nt(jnp.concatenate(left, axis=0), c0_ref[...])
    left = [r0[:inner] * x for x in split(b)]
    along = dot_nt(jnp.concatenate(left, axis=0), cy_ref[...])
    total = both[:lines] + both[lines : 2 * lines]
    u_scr[pl.ds(0, inner), :] = total[:inner] + (along[:inner] + along[inner:])
    u_scr[pl.ds(inner, lines - inner), :] = total[inner:]
    v_scr[...] = both[2 * lines : 3 * lines] + both[3 * lines :]

    block = chunk * rows
    for s in range(levels // chunk):
        product = []
        for m in range(members):
            for n in range(chunk):
                k = s * chunk + n
                u = u_scr[pl.ds(k * rows, rows), :]
                v = v_scr[pl.ds(k * rows, rows), :]
                product.append(u * pert_ref[m, 0, k].astype(F32) + v * pert_ref[m, 1, k].astype(F32))
        high, lower = split(jnp.concatenate(product, axis=0))
        got = dot_nn(high, table) + dot_nn(lower, table)
        for m in range(members):
            f_scr[pl.ds(m * inner + s * block, block), :] = got[m * block : (m + 1) * block]

    out = {}

    def add(i, value):
        low, w0, w1 = weights_x(i, ratio)
        for at, w in ((low, w0), (low + 1, w1)):
            out[at] = w * value if at not in out else out[at] + w * value

    for side in range(2):
        u = u_scr[pl.ds(inner + side * levels, levels), :]
        v = v_scr[pl.ds(inner + side * levels, levels), :]
        product = []
        for m in range(members):
            halo = []
            for part in range(2):
                e, o = even_ref[m, part], odd_ref[m, part]
                halo.append(jnp.where(even, o, e) if side == 0 else jnp.where(even, e, o))
            product.append(u * halo[0] + v * halo[1])
        high, lower = split(jnp.concatenate(product, axis=0))
        got = dot_nn(high, table) + dot_nn(lower, table)
        add(-1 if side == 0 else rows, got)
    for i in range(rows):
        add(i, f_scr[pl.ds(i, pairs, stride=rows), :])
    held = {r: mask_row(value * scale, r, coarse_rows, region, regions) for r, value in out.items()}
    held = smooth(
        held, range(-HALO, coarse_rows + HALO), coarse_rows, region, regions, twice_ref[...], once_ref[...]
    )
    for r in range(coarse_rows):
        own_out[r] = held[r]
    for k in range(HALO):
        before, after = held[k - HALO], held[coarse_rows + k]
        a_out[k] = jnp.where(even, after, before)
        b_out[k] = jnp.where(even, before, after)


def backward(q_terms, kind, value, weight, tables_y, pert, halo_even, halo_odd, hot, scale, coarse_rows, coarse_columns):
    members, _, levels, rows, columns = pert.shape
    pairs = members * levels
    outs = [jax.ShapeDtypeStruct((n, pairs, coarse_columns), F32) for n in (coarse_rows, HALO, HALO)]
    return pl.pallas_call(
        functools.partial(backward_kernel, scale, 4 if levels % 4 == 0 else 1, len(q_terms)),
        out_shape=outs,
        scratch_shapes=[
            pltpu.VMEM((levels * rows + 2 * levels, columns), F32),
            pltpu.VMEM((levels * rows + 2 * levels, columns), F32),
            pltpu.VMEM((pairs * rows, coarse_columns), F32),
        ],
        compiler_params=params(28),
        name="adjoint_to_coarse",
    )(*q_terms, kind, value, weight, *tables_y, pert, halo_even, halo_odd, *hot)


def join_kernel(coarse_rows, own_ref, even_ref, odd_ref, out_ref):
    even = lax.rem(lax.axis_index("reg"), 2) == 0
    pairs = own_ref.shape[1]
    for r in range(coarse_rows):
        total = own_ref[r]
        if r < HALO:
            total = total + jnp.where(even, odd_ref[r], even_ref[r])
        k = r - (coarse_rows - HALO)
        if k >= 0:
            total = total + jnp.where(even, even_ref[k], odd_ref[k])
        out_ref[pl.ds(r, pairs, stride=coarse_rows), :] = total


def join(own, got_even, got_odd):
    coarse_rows, pairs, columns = own.shape
    return pl.pallas_call(
        functools.partial(join_kernel, coarse_rows),
        out_shape=jax.ShapeDtypeStruct((pairs * coarse_rows, columns), F32),
        compiler_params=params(16),
        name="join_rows",
    )(own, got_even, got_odd)


def local(alpha, perturbation, obs_cell, obs_kind, obs_value, obs_weight):
    members, levels, coarse_rows, coarse_columns = alpha.shape
    _, _, _, rows, columns = perturbation.shape
    scale = 1.0 / math.sqrt(members * lax.axis_size("mem"))
    flat = alpha.reshape(-1, coarse_columns)
    cell, kind, value, weight = (x.reshape(1, -1) for x in (obs_cell, obs_kind, obs_value, obs_weight))
    down = down_weights(coarse_columns, columns)
    flat_odd = swap_odd(flat)
    flat_even = swap_even(flat)
    pack_a, pack_b = pack(perturbation)
    halo_odd = swap_odd(pack_b)
    halo_even = swap_even(pack_a)
    hot, along_y = tables(cell, kind, levels, rows, columns, coarse_columns)
    q, edge_fine = forward(flat, flat_even, flat_odd, along_y, perturbation, hot, scale)
    q = edge(q, edge_fine, halo_even, halo_odd, hot, members, levels)
    terms = others(q, "mem")
    own, send_a, send_b = backward(
        terms, kind, value, weight, (down, *along_y[1:]), perturbation, halo_even, halo_odd, hot, scale,
        coarse_rows, coarse_columns,
    )
    got_odd = swap_odd(send_b)
    got_even = swap_even(send_a)
    return join(own, got_even, got_odd).reshape(alpha.shape)


def solution(mesh):
    return jax.shard_map(
        local,
        mesh=mesh,
        in_specs=(
            P("mem", None, "reg", None),
            P("mem", None, None, "reg", None),
            P("reg"),
            P("reg"),
            P("reg"),
            P("reg"),
        ),
        out_specs=P("mem", None, "reg", None),
        check_vma=False,
    )
```

```python
import functools
import math

import jax
import jax.numpy as jnp
from jax import lax
from jax.experimental import pallas as pl
from jax.experimental.pallas import tpu as pltpu
from jax.sharding import PartitionSpec as P


PASSES = 2
HALO = PASSES + 1
DIFFUSE = 0.2
CENTRE = round((1.0 - 4.0 * DIFFUSE) / DIFFUSE)
F32 = jnp.float32
BF16 = jnp.bfloat16


def params(mib):
    return pltpu.CompilerParams(vmem_limit_bytes=mib << 20)


def swap_pairs(n, odd):
    pairs = []
    for i in range(1 if odd else 0, n - 1, 2):
        pairs += [(i, i + 1), (i + 1, i)]
    return pairs


def swap_even(value):
    return lax.ppermute(value, "reg", swap_pairs(lax.axis_size("reg"), False))


def swap_odd(value):
    return lax.ppermute(value, "reg", swap_pairs(lax.axis_size("reg"), True))


def others(value, axis):
    n = lax.axis_size(axis)
    stride = 1
    rounds = []
    while stride < n:
        left = n // stride
        radix = 4 if left % 4 == 0 else 2 if left % 2 == 0 else left
        sends = []
        for k in range(1, radix):
            pairs = []
            for i in range(n):
                digit = (i // stride) % radix
                other = digit ^ k if radix in (2, 4) else (digit + k) % radix
                pairs.append((i, i + (other - digit) * stride))
            sends.append(pairs)
        rounds.append(sends)
        stride *= radix
    for number, sends in enumerate(rounds):
        got = []
        for pairs in sends:
            got.append(lax.ppermute(value, axis, pairs))
        if number == len(rounds) - 1:
            return [value] + got
        for part in got:
            value = value + part
    return [value]


def split(x):
    high = x.astype(BF16)
    return high, (x - high.astype(F32)).astype(BF16)


def dot_nn(a, b):
    return lax.dot_general(a, b, (((1,), (0,)), ((), ())), preferred_element_type=F32)


def dot_nt(a, b):
    return lax.dot_general(a, b, (((1,), (1,)), ((), ())), preferred_element_type=F32)


def iota(shape, dim):
    return lax.broadcasted_iota(jnp.int32, shape, dim)


def table_y(coarse, fine, coarse_dim):
    shape = (coarse, fine) if coarse_dim == 0 else (fine, coarse)
    ratio = fine // coarse
    at = (iota(shape, 1 - coarse_dim).astype(F32) + 0.5) / ratio - 0.5
    return jnp.maximum(0.0, 1.0 - jnp.abs(at - iota(shape, coarse_dim).astype(F32))).astype(BF16)


def weights_x(i, ratio):
    at = (i + 0.5) / ratio - 0.5
    low = math.floor(at)
    return low, 1.0 - (at - low), at - low


def filters(columns):
    row, column = iota((columns, columns), 0), iota((columns, columns), 1)
    near = jnp.abs(row - column)
    once = jnp.where(near == 0, CENTRE, jnp.where(near == 1, 1.0, 0.0)).astype(BF16)
    twice = dot_nn(once, once).astype(BF16)
    once = once + once
    return jnp.concatenate([twice, twice], axis=0), jnp.concatenate([once, once], axis=0)


def smooth(rows, wanted, coarse_rows, region, regions, twice, once):
    pairs = next(iter(rows.values())).shape[0]

    def both(values):
        high, lower = split(jnp.concatenate(values, axis=0))
        return jnp.concatenate([high, lower], axis=1)

    def total(*names):
        found = [rows[n] for n in names if n in rows]
        return functools.reduce(jnp.add, found) if found else None

    mids = [r for r in wanted if r in rows]
    at_mid = dot_nn(both([rows[r] for r in mids]), twice)
    sides = [r for r in wanted if total(r - 1, r + 1) is not None]
    at_side = dot_nn(both([total(r - 1, r + 1) for r in sides]), once)
    out = {}
    for r in wanted:
        terms = []
        if r in mids:
            k = mids.index(r)
            terms.append(at_mid[k * pairs : (k + 1) * pairs])
            around = 2.0
            if r == 0:
                around = jnp.where(region > 0, 2.0, 1.0)
            elif r == coarse_rows - 1:
                around = jnp.where(region < regions - 1, 2.0, 1.0)
            terms.append(around * rows[r])
        if r in sides:
            k = sides.index(r)
            terms.append(at_side[k * pairs : (k + 1) * pairs])
        far = total(r - 2, r + 2)
        if far is not None:
            terms.append(far)
        out[r] = (DIFFUSE * DIFFUSE) * functools.reduce(jnp.add, terms)
    return out


def mask_row(value, index, coarse_rows, region, regions):
    if index < 0:
        return jnp.where(region * coarse_rows + index >= 0, value, 0.0)
    if index >= coarse_rows:
        return jnp.where(region * coarse_rows + index < regions * coarse_rows, value, 0.0)
    return value


def sides():
    odd = lax.rem(lax.axis_index("reg"), 2)
    return 1 - odd, odd


def decode(cell, rows, columns):
    plane = rows * columns
    level = cell // plane
    rest = cell - level * plane
    row = rest // columns
    return level, row, rest - row * columns


def down_kernel(down_ref):
    fine, coarse = down_ref.shape
    down_ref[...] = table_y(coarse, fine, 1)


def down_weights(coarse, fine):
    return pl.pallas_call(
        down_kernel,
        out_shape=jax.ShapeDtypeStruct((fine, coarse), BF16),
        compiler_params=params(16),
        cost_estimate=pl.CostEstimate(flops=1160000000, bytes_accessed=1 << 20, transcendentals=0),
        name="down_weights",
    )()


def pack_kernel(last_parity, pert_ref, out_ref):
    members, parts, levels, rows, columns = pert_ref.shape
    half = rows // 2
    last = jnp.where(lax.rem(lax.axis_index("reg"), 2) == last_parity, 1, 0)
    shape = (levels, levels * half)
    wanted = iota(shape, 0) * half + last * (half - 1)
    chooser = jnp.where(iota(shape, 1) == wanted, 1.0, 0.0).astype(BF16)
    inside = pl.ds(pl.multiple_of(last * half, half), half)
    for m in range(members):
        for part in range(parts):
            block = pert_ref[m, part, :, inside, :].reshape(levels * half, columns)
            out_ref[m, part] = dot_nn(chooser, block)


def pack(pert, last_parity):
    members, parts, levels, _, columns = pert.shape
    return pl.pallas_call(
        functools.partial(pack_kernel, last_parity),
        out_shape=jax.ShapeDtypeStruct((members, parts, levels, columns), F32),
        compiler_params=params(16),
    )(pert)


def tables_kernel(
    levels, rows, columns, cell_ref, kind_ref, r0_ref, ru_ref, rv_ref, c0_ref, cy_ref, up_ref, twice_ref, once_ref
):
    coarse = twice_ref.shape[1]
    up = table_y(coarse, columns, 0)
    up_ref[...] = jnp.concatenate([up, up], axis=0)
    twice_ref[...], once_ref[...] = filters(coarse)
    cell, kind = cell_ref[...], kind_ref[...]
    level, row, column = decode(cell, rows, columns)
    line = level * rows + row
    count = cell.shape[1]
    inner = levels * rows
    minus = jnp.where(row > 0, line - 1, inner + level)
    plus = jnp.where(row < rows - 1, line + 1, inner + levels + level)
    none = jnp.full_like(line, -1)
    minus_u = jnp.where(kind == 3, minus, none)
    plus_u = jnp.where(kind == 3, plus, none)
    here_v = jnp.where((kind == 1) | (kind == 3), line, none)
    minus_v = jnp.where(kind == 2, minus, none)
    plus_v = jnp.where(kind == 2, plus, none)
    step = 32

    def lines(k, _):
        start = pl.multiple_of(k * step, step)
        at = iota((step, count), 0) + start
        ru = jnp.where(at == plus_u, 0.5, jnp.where(at == minus_u, -0.5, 0.0))
        rv = jnp.where(at == plus_v, 0.5, jnp.where(at == minus_v, -0.5, jnp.where(at == here_v, 1.0, 0.0)))
        r0 = jnp.where(at == line, 1.0, 0.0)
        ru_ref[pl.ds(start, step), :] = ru.astype(BF16)
        rv_ref[pl.ds(start, step), :] = rv.astype(BF16)
        r0_ref[pl.ds(start, step), :] = r0.astype(BF16)
        return 0

    lax.fori_loop(0, (inner + 2 * levels) // step, lines, 0)

    def cells(k, _):
        start = pl.multiple_of(k * step, step)
        at = iota((step, count), 0) + start
        c0_ref[pl.ds(start, step), :] = jnp.where(at == column, 1.0, 0.0).astype(BF16)
        cy = jnp.where(at == column + 1, 0.5, jnp.where(at == column - 1, -0.5, 0.0))
        cy_ref[pl.ds(start, step), :] = cy.astype(BF16)
        return 0

    lax.fori_loop(0, columns // step, cells, 0)


def tables(cell, kind, levels, rows, columns, coarse):
    count = cell.shape[1]
    lines = levels * rows + 2 * levels
    shapes = [(n, count) for n in (lines, lines, lines, columns, columns)]
    shapes += [(2 * coarse, columns), (2 * coarse, coarse), (2 * coarse, coarse)]
    made = pl.pallas_call(
        functools.partial(tables_kernel, levels, rows, columns),
        out_shape=[jax.ShapeDtypeStruct(shape, BF16) for shape in shapes],
        compiler_params=params(16),
        name="one_hots",
    )(cell, kind)
    return made[:5], made[5:]


def forward_kernel(
    scale, chunk,
    own_ref, even_ref, odd_ref, up_ref, twice_ref, once_ref, pert_ref, r0_ref, ru_ref, rv_ref, c0_ref, cy_ref,
    q_ref, edge_ref,
    fine_in, fine_scr, t_scr,
):
    region = lax.axis_index("reg")
    regions = lax.axis_size("reg")
    members, _, levels, rows, _ = pert_ref.shape
    pairs = members * levels
    coarse_rows = own_ref.shape[0] // pairs
    ratio = rows // coarse_rows
    block = chunk * rows
    inner = levels * rows
    even = lax.rem(region, 2) == 0
    table = up_ref[...]
    rows_in = {r: own_ref[pl.ds(r, pairs, stride=coarse_rows), :] for r in range(coarse_rows)}
    for k in range(HALO):
        low = coarse_rows - HALO + k
        e = even_ref[pl.ds(low, pairs, stride=coarse_rows), :]
        o = odd_ref[pl.ds(low, pairs, stride=coarse_rows), :]
        rows_in[k - HALO] = jnp.where(even, o, e)
        e = even_ref[pl.ds(k, pairs, stride=coarse_rows), :]
        o = odd_ref[pl.ds(k, pairs, stride=coarse_rows), :]
        rows_in[coarse_rows + k] = jnp.where(even, e, o)
    rows_in = smooth(
        rows_in, range(-1, coarse_rows + 1), coarse_rows, region, regions, twice_ref[...], once_ref[...]
    )
    rows_in = {r: mask_row(value, r, coarse_rows, region, regions) for r, value in rows_in.items()}
    for i in range(-1, rows + 1):
        low, w0, w1 = weights_x(i, ratio)
        value = (w0 * rows_in[low] + w1 * rows_in[low + 1]) * scale
        if 0 <= i < rows:
            fine_in[pl.ds(i, pairs, stride=rows), :] = value
        else:
            high, lower = split(value)
            got = dot_nn(jnp.concatenate([high, lower], axis=1), table)
            edge_ref[0 if i < 0 else 1] = got

    for step in range(levels // chunk):
        parts = []
        for m in range(members):
            parts.append(fine_in[pl.ds(m * inner + step * block, block), :])
        high, lower = split(jnp.concatenate(parts, axis=0))
        fine_scr[step % 2] = dot_nn(jnp.concatenate([high, lower], axis=1), table)
        for k in range(chunk):
            u = v = None
            for m in range(members):
                fine = fine_scr[step % 2, pl.ds(m * block + k * rows, rows), :]
                pu = fine * pert_ref[m, 0, step * chunk + k].astype(F32)
                pv = fine * pert_ref[m, 1, step * chunk + k].astype(F32)
                u = pu if u is None else u + pu
                v = pv if v is None else v + pv
            for n, value in enumerate((*split(u), *split(v))):
                t_scr[pl.ds(n * inner + step * block + k * rows, rows), :] = value

    count = r0_ref.shape[1]
    width = min(256, count)
    for k in range(count // width):
        at = pl.ds(k * width, width)
        z = dot_nn(t_scr[...], c0_ref[:, at])
        zy = dot_nn(t_scr[pl.ds(0, 2 * inner), :], cy_ref[:, at])
        zu = z[:inner] + z[inner : 2 * inner]
        zv = z[2 * inner : 3 * inner] + z[3 * inner :]
        zy = zy[:inner] + zy[inner:]
        inside = pl.ds(0, inner)
        r0 = r0_ref[inside, at].astype(F32)
        q_ref[pl.ds(0, 1), at] = jnp.sum(r0 * zu, axis=0, keepdims=True)
        q_ref[pl.ds(1, 1), at] = jnp.sum(rv_ref[inside, at].astype(F32) * zv, axis=0, keepdims=True)
        q_ref[pl.ds(2, 1), at] = jnp.sum(ru_ref[inside, at].astype(F32) * zu, axis=0, keepdims=True)
        q_ref[pl.ds(3, 1), at] = jnp.sum(r0 * zy, axis=0, keepdims=True)


def forward(own, got_even, got_odd, weight, pert, hot, scale):
    up, twice, once = weight
    members, _, levels, rows, columns = pert.shape
    pairs, coarse_columns = members * levels, own.shape[1]
    chunk = 4 if levels % 4 == 0 else 1
    count = hot[0].shape[1]
    return pl.pallas_call(
        functools.partial(forward_kernel, scale, chunk),
        out_shape=[jax.ShapeDtypeStruct((4, count), F32),
                   jax.ShapeDtypeStruct((2, pairs, columns), F32)],
        scratch_shapes=[
            pltpu.VMEM((pairs * rows, coarse_columns), F32),
            pltpu.VMEM((2, members * chunk * rows, columns), F32),
            pltpu.VMEM((4 * levels * rows, columns), BF16),
        ],
        compiler_params=params(28),
        name="increment_at_obs",
    )(own, got_even, got_odd, up, twice, once, pert, *hot)


def edge_kernel(members, levels, q_ref, fine_ref, even_ref, odd_ref, ru_ref, rv_ref, c0_ref, out_ref):
    side = sides()
    lines, _ = ru_ref.shape
    inner = lines - 2 * levels
    table = []
    for part in range(2):
        for near, halo_ref in zip(side, (even_ref, odd_ref)):
            total = None
            for m in range(members):
                term = fine_ref[near, pl.ds(m * levels, levels), :] * halo_ref[m, part]
                total = term if total is None else total + term
            table.append(total)
    high, lower = split(jnp.concatenate(table, axis=0))
    z = dot_nn(jnp.concatenate([high, lower], axis=0), c0_ref[...])
    z = z[: 4 * levels] + z[4 * levels :]
    for n, ref in ((0, ru_ref), (2, rv_ref)):
        total = q_ref[pl.ds(2 - n // 2, 1), :]
        for k in range(2):
            here = pl.ds(pl.multiple_of(inner + side[k] * levels, levels), levels)
            part = z[(n + k) * levels : (n + k + 1) * levels]
            total = total + jnp.sum(ref[here, :].astype(F32) * part, axis=0, keepdims=True)
        out_ref[pl.ds(2 - n // 2, 1), :] = total
    out_ref[pl.ds(0, 1), :] = q_ref[pl.ds(0, 1), :]
    out_ref[pl.ds(3, 1), :] = q_ref[pl.ds(3, 1), :]


def edge(q, fine, halo_even, halo_odd, hot, members, levels):
    _, ru, rv, c0, _ = hot
    return pl.pallas_call(
        functools.partial(edge_kernel, members, levels),
        out_shape=jax.ShapeDtypeStruct(q.shape, F32),
        compiler_params=params(16),
        name="edge_at_obs",
    )(q, fine, halo_even, halo_odd, ru, rv, c0)


def backward_kernel(scale, chunk, terms, *refs):
    q_refs = refs[:terms]
    (kind_ref, value_ref, weight_ref, down_ref, twice_ref, once_ref, pert_ref, even_ref, odd_ref,
     r0_ref, ru_ref, rv_ref, c0_ref, cy_ref,
     own_out, a_out, b_out,
     u_scr, v_scr, f_scr) = refs[terms:]
    region = lax.axis_index("reg")
    regions = lax.axis_size("reg")
    members, _, levels, rows, _ = pert_ref.shape
    coarse_rows, pairs, _ = own_out.shape
    ratio = rows // coarse_rows
    inner = levels * rows
    even = lax.rem(region, 2) == 0

    q = q_refs[0][...]
    for ref in q_refs[1:]:
        q = q + ref[...]
    q0, q1, q2, q3 = (q[n : n + 1] for n in range(4))
    kind = kind_ref[...]
    seen = jnp.where(kind == 0, q0, jnp.where(kind == 1, q1, jnp.where(kind == 2, q1 - q3, q0 * q2 + q1 * q3)))
    misfit = weight_ref[...] * (seen - value_ref[...])
    zero = jnp.zeros_like(misfit)
    a = jnp.where(kind == 0, misfit, jnp.where(kind == 3, misfit * q2, zero))
    b = jnp.where(kind == 2, -misfit, jnp.where(kind == 3, misfit * q1, zero))
    c = jnp.where(kind == 3, misfit * q0, zero)
    g = jnp.where(kind == 3, misfit * q3, jnp.where(kind == 0, zero, misfit))
    r0, ru, rv = r0_ref[...], ru_ref[...], rv_ref[...]
    lines = r0.shape[0]
    left = [r0 * x + ru * y for x, y in zip(split(a), split(c))] + [rv * x for x in split(g)]
    left = jnp.concatenate(left, axis=0)
    left_y = jnp.concatenate([r0[:inner] * x for x in split(b)], axis=0)
    both = dot_nt(left, c0_ref[...])
    along = dot_nt(left_y, cy_ref[...])
    total = both[:lines] + both[lines : 2 * lines]
    u_scr[pl.ds(0, inner), :] = total[:inner] + (along[:inner] + along[inner:])
    u_scr[pl.ds(inner, lines - inner), :] = total[inner:]
    v_scr[...] = both[2 * lines : 3 * lines] + both[3 * lines :]

    def project(products):
        high, lower = split(jnp.concatenate(products, axis=0))
        return dot_nn(high, down_ref[...]) + dot_nn(lower, down_ref[...])

    block = chunk * rows
    for s in range(levels // chunk):
        products = []
        for m in range(members):
            for k in range(s * chunk, (s + 1) * chunk):
                here = pl.ds(k * rows, rows)
                pu, pv = pert_ref[m, 0, k].astype(F32), pert_ref[m, 1, k].astype(F32)
                products.append(u_scr[here, :] * pu + v_scr[here, :] * pv)
        got = project(products)
        for m in range(members):
            f_scr[pl.ds(m * inner + s * block, block), :] = got[m * block : (m + 1) * block]

    edges = {}
    for n in range(2):
        rim = pl.ds(inner + n * levels, levels)
        u, v = u_scr[rim, :], v_scr[rim, :]
        found = []
        for m in range(members):
            halo = []
            for part in range(2):
                x, y = even_ref[m, part], odd_ref[m, part]
                halo.append(jnp.where(even, y, x) if n == 0 else jnp.where(even, x, y))
            found.append(u * halo[0] + v * halo[1])
        edges[-1 if n == 0 else rows] = project(found)

    held = {}
    for i in range(-1, rows + 1):
        value = edges[i] if i in edges else f_scr[pl.ds(i, pairs, stride=rows), :]
        low, w0, w1 = weights_x(i, ratio)
        for at, w in ((low, w0), (low + 1, w1)):
            held[at] = w * value if at not in held else held[at] + w * value
    held = {r: mask_row(value * scale, r, coarse_rows, region, regions) for r, value in held.items()}
    held = smooth(
        held, range(-HALO, coarse_rows + HALO), coarse_rows, region, regions, twice_ref[...], once_ref[...]
    )
    for r in range(coarse_rows):
        own_out[r] = held[r]
    for k in range(HALO):
        before, after = held[k - HALO], held[coarse_rows + k]
        a_out[k] = jnp.where(even, after, before)
        b_out[k] = jnp.where(even, before, after)


def backward(q_terms, kind, value, weight, tables_y, pert, halo_even, halo_odd, hot, scale, coarse_rows, coarse_columns):
    members, _, levels, rows, columns = pert.shape
    pairs = members * levels
    outs = [jax.ShapeDtypeStruct((n, pairs, coarse_columns), F32) for n in (coarse_rows, HALO, HALO)]
    return pl.pallas_call(
        functools.partial(backward_kernel, scale, 4 if levels % 4 == 0 else 1, len(q_terms)),
        out_shape=outs,
        scratch_shapes=[
            pltpu.VMEM((levels * rows + 2 * levels, columns), F32),
            pltpu.VMEM((levels * rows + 2 * levels, columns), F32),
            pltpu.VMEM((pairs * rows, coarse_columns), F32),
        ],
        compiler_params=params(28),
        name="adjoint_to_coarse",
    )(*q_terms, kind, value, weight, *tables_y, pert, halo_even, halo_odd, *hot)


def join_kernel(coarse_rows, own_ref, even_ref, odd_ref, out_hbm, out_scr, sem):
    even = lax.rem(lax.axis_index("reg"), 2) == 0
    pairs = own_ref.shape[1]
    chunks = sem.shape[0]
    some = pairs // chunks
    copies = []
    for n in range(chunks):
        here = pl.ds(n * some, some)
        for r in range(coarse_rows):
            total = own_ref[r, here, :]
            if r < HALO:
                total = total + jnp.where(even, odd_ref[r, here, :], even_ref[r, here, :])
            k = r - (coarse_rows - HALO)
            if k >= 0:
                total = total + jnp.where(even, even_ref[k, here, :], odd_ref[k, here, :])
            out_scr[pl.ds(n * some * coarse_rows + r, some, stride=coarse_rows), :] = total
        block = pl.ds(n * some * coarse_rows, some * coarse_rows)
        copy = pltpu.make_async_copy(out_scr.at[block], out_hbm.at[block], sem.at[n])
        copy.start()
        copies.append(copy)
    for copy in copies:
        copy.wait()


def join(own, got_even, got_odd):
    coarse_rows, pairs, columns = own.shape
    chunks = 4 if pairs % 32 == 0 else 1
    vmem = pl.BlockSpec(memory_space=pltpu.VMEM)
    return pl.pallas_call(
        functools.partial(join_kernel, coarse_rows),
        in_specs=[vmem, vmem, vmem],
        out_specs=pl.BlockSpec(memory_space=pltpu.HBM),
        out_shape=jax.ShapeDtypeStruct((pairs * coarse_rows, columns), F32),
        scratch_shapes=[
            pltpu.VMEM((pairs * coarse_rows, columns), F32),
            pltpu.SemaphoreType.DMA((chunks,)),
        ],
        compiler_params=params(16),
        name="join_rows",
    )(own, got_even, got_odd)


def local(alpha, perturbation, obs_cell, obs_kind, obs_value, obs_weight):
    members, levels, coarse_rows, coarse_columns = alpha.shape
    _, _, _, rows, columns = perturbation.shape
    scale = 1.0 / math.sqrt(members * lax.axis_size("mem"))
    flat = alpha.reshape(-1, coarse_columns)
    cell, kind, value, weight = (x.reshape(1, -1) for x in (obs_cell, obs_kind, obs_value, obs_weight))
    down = down_weights(coarse_columns, columns)
    flat_odd = swap_odd(flat)
    flat_even = swap_even(flat)
    packed = pack(perturbation, 1)
    halo_odd = swap_odd(packed)
    packed = pack(perturbation, 0)
    halo_even = swap_even(packed)
    hot, along_y = tables(cell, kind, levels, rows, columns, coarse_columns)
    q, edge_fine = forward(flat, flat_even, flat_odd, along_y, perturbation, hot, scale)
    q = edge(q, edge_fine, halo_even, halo_odd, hot, members, levels)
    terms = others(q, "mem")
    own, send_a, send_b = backward(
        terms, kind, value, weight, (down, *along_y[1:]), perturbation, halo_even, halo_odd, hot, scale,
        coarse_rows, coarse_columns,
    )
    got_odd = swap_odd(send_b)
    got_even = swap_even(send_a)
    return join(own, got_even, got_odd).reshape(alpha.shape)


def solution(mesh):
    return jax.shard_map(
        local,
        mesh=mesh,
        in_specs=(
            P("mem", None, "reg", None),
            P("mem", None, None, "reg", None),
            P("reg"),
            P("reg"),
            P("reg"),
            P("reg"),
        ),
        out_specs=P("mem", None, "reg", None),
        check_vma=False,
    )
```

```python
import functools
import math

import jax
import jax.numpy as jnp
from jax import lax
from jax.experimental import pallas as pl
from jax.experimental.pallas import tpu as pltpu
from jax.sharding import PartitionSpec as P


PASSES = 2
HALO = PASSES + 1
DIFFUSE = 0.2
CENTRE = round((1.0 - 4.0 * DIFFUSE) / DIFFUSE)
F32 = jnp.float32
BF16 = jnp.bfloat16


def params(mib):
    return pltpu.CompilerParams(vmem_limit_bytes=mib << 20)


def swap_pairs(n, odd):
    pairs = []
    for i in range(1 if odd else 0, n - 1, 2):
        pairs += [(i, i + 1), (i + 1, i)]
    return pairs


def swap_even(value):
    return lax.ppermute(value, "reg", swap_pairs(lax.axis_size("reg"), False))


def swap_odd(value):
    return lax.ppermute(value, "reg", swap_pairs(lax.axis_size("reg"), True))


def others(value, axis):
    n = lax.axis_size(axis)
    stride = 1
    rounds = []
    while stride < n:
        left = n // stride
        radix = 4 if left % 4 == 0 else 2 if left % 2 == 0 else left
        sends = []
        for k in range(1, radix):
            pairs = []
            for i in range(n):
                digit = (i // stride) % radix
                other = digit ^ k if radix in (2, 4) else (digit + k) % radix
                pairs.append((i, i + (other - digit) * stride))
            sends.append(pairs)
        rounds.append(sends)
        stride *= radix
    for number, sends in enumerate(rounds):
        got = []
        for pairs in sends:
            got.append(lax.ppermute(value, axis, pairs))
        if number == len(rounds) - 1:
            return [value] + got
        for part in got:
            value = value + part
    return [value]


def split(x):
    high = x.astype(BF16)
    return high, (x - high.astype(F32)).astype(BF16)


def dot_nn(a, b):
    return lax.dot_general(a, b, (((1,), (0,)), ((), ())), preferred_element_type=F32)


def dot_nt(a, b):
    return lax.dot_general(a, b, (((1,), (1,)), ((), ())), preferred_element_type=F32)


def iota(shape, dim):
    return lax.broadcasted_iota(jnp.int32, shape, dim)


def table_y(coarse, fine, coarse_dim):
    shape = (coarse, fine) if coarse_dim == 0 else (fine, coarse)
    ratio = fine // coarse
    at = (iota(shape, 1 - coarse_dim).astype(F32) + 0.5) / ratio - 0.5
    return jnp.maximum(0.0, 1.0 - jnp.abs(at - iota(shape, coarse_dim).astype(F32))).astype(BF16)


def weights_x(i, ratio):
    at = (i + 0.5) / ratio - 0.5
    low = math.floor(at)
    return low, 1.0 - (at - low), at - low


def filters(columns):
    row, column = iota((columns, columns), 0), iota((columns, columns), 1)
    near = jnp.abs(row - column)
    once = jnp.where(near == 0, CENTRE, jnp.where(near == 1, 1.0, 0.0)).astype(BF16)
    twice = dot_nn(once, once).astype(BF16)
    once = once + once
    return jnp.concatenate([twice, twice], axis=0), jnp.concatenate([once, once], axis=0)


def smooth(rows, wanted, coarse_rows, region, regions, twice, once):
    pairs = next(iter(rows.values())).shape[0]

    def both(values):
        high, lower = split(jnp.concatenate(values, axis=0))
        return jnp.concatenate([high, lower], axis=1)

    def total(*names):
        found = [rows[n] for n in names if n in rows]
        return functools.reduce(jnp.add, found) if found else None

    mids = [r for r in wanted if r in rows]
    at_mid = dot_nn(both([rows[r] for r in mids]), twice)
    sides = [r for r in wanted if total(r - 1, r + 1) is not None]
    at_side = dot_nn(both([total(r - 1, r + 1) for r in sides]), once)
    out = {}
    for r in wanted:
        terms = []
        if r in mids:
            k = mids.index(r)
            terms.append(at_mid[k * pairs : (k + 1) * pairs])
            around = 2.0
            if r == 0:
                around = jnp.where(region > 0, 2.0, 1.0)
            elif r == coarse_rows - 1:
                around = jnp.where(region < regions - 1, 2.0, 1.0)
            terms.append(around * rows[r])
        if r in sides:
            k = sides.index(r)
            terms.append(at_side[k * pairs : (k + 1) * pairs])
        far = total(r - 2, r + 2)
        if far is not None:
            terms.append(far)
        out[r] = (DIFFUSE * DIFFUSE) * functools.reduce(jnp.add, terms)
    return out


def mask_row(value, index, coarse_rows, region, regions):
    if index < 0:
        return jnp.where(region * coarse_rows + index >= 0, value, 0.0)
    if index >= coarse_rows:
        return jnp.where(region * coarse_rows + index < regions * coarse_rows, value, 0.0)
    return value


def sides():
    odd = lax.rem(lax.axis_index("reg"), 2)
    return 1 - odd, odd


def decode(cell, rows, columns):
    plane = rows * columns
    level = cell // plane
    rest = cell - level * plane
    row = rest // columns
    return level, row, rest - row * columns


def down_kernel(down_ref):
    fine, coarse = down_ref.shape
    down_ref[...] = table_y(coarse, fine, 1)


def down_weights(coarse, fine):
    return pl.pallas_call(
        down_kernel,
        out_shape=jax.ShapeDtypeStruct((fine, coarse), BF16),
        compiler_params=params(16),
        cost_estimate=pl.CostEstimate(flops=1160000000, bytes_accessed=1 << 20, transcendentals=0),
        name="down_weights",
    )()


def pack_kernel(last_parity, pert_ref, out_ref):
    members, parts, levels, rows, columns = pert_ref.shape
    half = rows // 2
    last = jnp.where(lax.rem(lax.axis_index("reg"), 2) == last_parity, 1, 0)
    shape = (levels, levels * half)
    wanted = iota(shape, 0) * half + last * (half - 1)
    chooser = jnp.where(iota(shape, 1) == wanted, 1.0, 0.0).astype(BF16)
    inside = pl.ds(pl.multiple_of(last * half, half), half)
    for m in range(members):
        for part in range(parts):
            block = pert_ref[m, part, :, inside, :].reshape(levels * half, columns)
            out_ref[m, part] = dot_nn(chooser, block)


def pack(pert, last_parity):
    members, parts, levels, _, columns = pert.shape
    return pl.pallas_call(
        functools.partial(pack_kernel, last_parity),
        out_shape=jax.ShapeDtypeStruct((members, parts, levels, columns), F32),
        compiler_params=params(16),
    )(pert)


def tables_kernel(
    levels, rows, columns, cell_ref, kind_ref, r0_ref, ru_ref, rv_ref, c0_ref, cy_ref, up_ref, twice_ref, once_ref
):
    coarse = twice_ref.shape[1]
    up = table_y(coarse, columns, 0)
    up_ref[...] = jnp.concatenate([up, up], axis=0)
    twice_ref[...], once_ref[...] = filters(coarse)
    cell, kind = cell_ref[...], kind_ref[...]
    level, row, column = decode(cell, rows, columns)
    line = level * rows + row
    count = cell.shape[1]
    inner = levels * rows
    minus = jnp.where(row > 0, line - 1, inner + level)
    plus = jnp.where(row < rows - 1, line + 1, inner + levels + level)
    none = jnp.full_like(line, -1)
    minus_u = jnp.where(kind == 3, minus, none)
    plus_u = jnp.where(kind == 3, plus, none)
    here_v = jnp.where((kind == 1) | (kind == 3), line, none)
    minus_v = jnp.where(kind == 2, minus, none)
    plus_v = jnp.where(kind == 2, plus, none)
    step = 32

    def lines(k, _):
        start = pl.multiple_of(k * step, step)
        at = iota((step, count), 0) + start
        ru = jnp.where(at == plus_u, 0.5, jnp.where(at == minus_u, -0.5, 0.0))
        rv = jnp.where(at == plus_v, 0.5, jnp.where(at == minus_v, -0.5, jnp.where(at == here_v, 1.0, 0.0)))
        r0 = jnp.where(at == line, 1.0, 0.0)
        ru_ref[pl.ds(start, step), :] = ru.astype(BF16)
        rv_ref[pl.ds(start, step), :] = rv.astype(BF16)
        r0_ref[pl.ds(start, step), :] = r0.astype(BF16)
        return 0

    lax.fori_loop(0, (inner + 2 * levels) // step, lines, 0)

    def cells(k, _):
        start = pl.multiple_of(k * step, step)
        at = iota((step, count), 0) + start
        c0_ref[pl.ds(start, step), :] = jnp.where(at == column, 1.0, 0.0).astype(BF16)
        cy = jnp.where(at == column + 1, 0.5, jnp.where(at == column - 1, -0.5, 0.0))
        cy_ref[pl.ds(start, step), :] = cy.astype(BF16)
        return 0

    lax.fori_loop(0, columns // step, cells, 0)


def tables(cell, kind, levels, rows, columns, coarse):
    count = cell.shape[1]
    lines = levels * rows + 2 * levels
    shapes = [(n, count) for n in (lines, lines, lines, columns, columns)]
    shapes += [(2 * coarse, columns), (2 * coarse, coarse), (2 * coarse, coarse)]
    made = pl.pallas_call(
        functools.partial(tables_kernel, levels, rows, columns),
        out_shape=[jax.ShapeDtypeStruct(shape, BF16) for shape in shapes],
        compiler_params=params(16),
        name="one_hots",
    )(cell, kind)
    return made[:5], made[5:]


def forward_kernel(
    scale, chunk,
    own_ref, even_ref, odd_ref, up_ref, twice_ref, once_ref, pert_ref, r0_ref, ru_ref, rv_ref, c0_ref, cy_ref,
    q_ref, edge_ref,
    fine_in, fine_scr, t_scr,
):
    region = lax.axis_index("reg")
    regions = lax.axis_size("reg")
    members, _, levels, rows, _ = pert_ref.shape
    pairs = members * levels
    coarse_rows = own_ref.shape[0] // pairs
    ratio = rows // coarse_rows
    block = chunk * rows
    inner = levels * rows
    even = lax.rem(region, 2) == 0
    table = up_ref[...]
    rows_in = {r: own_ref[pl.ds(r, pairs, stride=coarse_rows), :] for r in range(coarse_rows)}
    for k in range(HALO):
        low = coarse_rows - HALO + k
        e = even_ref[pl.ds(low, pairs, stride=coarse_rows), :]
        o = odd_ref[pl.ds(low, pairs, stride=coarse_rows), :]
        rows_in[k - HALO] = jnp.where(even, o, e)
        e = even_ref[pl.ds(k, pairs, stride=coarse_rows), :]
        o = odd_ref[pl.ds(k, pairs, stride=coarse_rows), :]
        rows_in[coarse_rows + k] = jnp.where(even, e, o)
    rows_in = smooth(
        rows_in, range(-1, coarse_rows + 1), coarse_rows, region, regions, twice_ref[...], once_ref[...]
    )
    rows_in = {r: mask_row(value, r, coarse_rows, region, regions) for r, value in rows_in.items()}
    for i in range(-1, rows + 1):
        low, w0, w1 = weights_x(i, ratio)
        value = (w0 * rows_in[low] + w1 * rows_in[low + 1]) * scale
        if 0 <= i < rows:
            fine_in[pl.ds(i, pairs, stride=rows), :] = value
        else:
            high, lower = split(value)
            got = dot_nn(jnp.concatenate([high, lower], axis=1), table)
            edge_ref[0 if i < 0 else 1] = got

    for step in range(levels // chunk):
        parts = []
        for m in range(members):
            parts.append(fine_in[pl.ds(m * inner + step * block, block), :])
        high, lower = split(jnp.concatenate(parts, axis=0))
        fine_scr[step % 2] = dot_nn(jnp.concatenate([high, lower], axis=1), table)
        for k in range(chunk):
            u = v = None
            for m in range(members):
                fine = fine_scr[step % 2, pl.ds(m * block + k * rows, rows), :]
                pu = fine * pert_ref[m, 0, step * chunk + k].astype(F32)
                pv = fine * pert_ref[m, 1, step * chunk + k].astype(F32)
                u = pu if u is None else u + pu
                v = pv if v is None else v + pv
            for n, value in enumerate((*split(u), *split(v))):
                t_scr[pl.ds(n * inner + step * block + k * rows, rows), :] = value

    count = r0_ref.shape[1]
    width = min(256, count)
    for k in range(count // width):
        at = pl.ds(k * width, width)
        z = dot_nn(t_scr[...], c0_ref[:, at])
        zy = dot_nn(t_scr[pl.ds(0, 2 * inner), :], cy_ref[:, at])
        zu = z[:inner] + z[inner : 2 * inner]
        zv = z[2 * inner : 3 * inner] + z[3 * inner :]
        zy = zy[:inner] + zy[inner:]
        inside = pl.ds(0, inner)
        r0 = r0_ref[inside, at].astype(F32)
        q_ref[pl.ds(0, 1), at] = jnp.sum(r0 * zu, axis=0, keepdims=True)
        q_ref[pl.ds(1, 1), at] = jnp.sum(rv_ref[inside, at].astype(F32) * zv, axis=0, keepdims=True)
        q_ref[pl.ds(2, 1), at] = jnp.sum(ru_ref[inside, at].astype(F32) * zu, axis=0, keepdims=True)
        q_ref[pl.ds(3, 1), at] = jnp.sum(r0 * zy, axis=0, keepdims=True)


def forward(own, got_even, got_odd, weight, pert, hot, scale):
    up, twice, once = weight
    members, _, levels, rows, columns = pert.shape
    pairs, coarse_columns = members * levels, own.shape[1]
    chunk = 4 if levels % 4 == 0 else 1
    count = hot[0].shape[1]
    return pl.pallas_call(
        functools.partial(forward_kernel, scale, chunk),
        out_shape=[jax.ShapeDtypeStruct((4, count), F32),
                   jax.ShapeDtypeStruct((2, pairs, columns), F32)],
        scratch_shapes=[
            pltpu.VMEM((pairs * rows, coarse_columns), F32),
            pltpu.VMEM((2, members * chunk * rows, columns), F32),
            pltpu.VMEM((4 * levels * rows, columns), BF16),
        ],
        compiler_params=params(28),
        name="increment_at_obs",
    )(own, got_even, got_odd, up, twice, once, pert, *hot)


def edge_kernel(members, levels, q_ref, fine_ref, even_ref, odd_ref, ru_ref, rv_ref, c0_ref, out_ref):
    side = sides()
    lines, _ = ru_ref.shape
    inner = lines - 2 * levels
    table = []
    for part in range(2):
        for near, halo_ref in zip(side, (even_ref, odd_ref)):
            total = None
            for m in range(members):
                term = fine_ref[near, pl.ds(m * levels, levels), :] * halo_ref[m, part]
                total = term if total is None else total + term
            table.append(total)
    high, lower = split(jnp.concatenate(table, axis=0))
    z = dot_nn(jnp.concatenate([high, lower], axis=0), c0_ref[...])
    z = z[: 4 * levels] + z[4 * levels :]
    for n, ref in ((0, ru_ref), (2, rv_ref)):
        total = q_ref[pl.ds(2 - n // 2, 1), :]
        for k in range(2):
            here = pl.ds(pl.multiple_of(inner + side[k] * levels, levels), levels)
            part = z[(n + k) * levels : (n + k + 1) * levels]
            total = total + jnp.sum(ref[here, :].astype(F32) * part, axis=0, keepdims=True)
        out_ref[pl.ds(2 - n // 2, 1), :] = total
    out_ref[pl.ds(0, 1), :] = q_ref[pl.ds(0, 1), :]
    out_ref[pl.ds(3, 1), :] = q_ref[pl.ds(3, 1), :]


def edge(q, fine, halo_even, halo_odd, hot, members, levels):
    _, ru, rv, c0, _ = hot
    return pl.pallas_call(
        functools.partial(edge_kernel, members, levels),
        out_shape=jax.ShapeDtypeStruct(q.shape, F32),
        compiler_params=params(16),
        name="edge_at_obs",
    )(q, fine, halo_even, halo_odd, ru, rv, c0)


def smooth_outside(held, before, twice_ref, once_ref):
    last = max(held) - 1
    rows = {r: jnp.where(before, held[r], held[last - r]) for r in range(-1, PASSES)}
    return smooth(rows, range(-HALO, 0), last + 1, 0, 1, twice_ref[...], once_ref[...])


def backward_kernel(scale, chunk, terms, *refs):
    q_refs = refs[:terms]
    (kind_ref, value_ref, weight_ref, down_ref, twice_ref, once_ref, pert_ref, even_ref, odd_ref,
     r0_ref, ru_ref, rv_ref, c0_ref, cy_ref,
     held_out, b_out,
     u_scr, v_scr, f_scr) = refs[terms:]
    region = lax.axis_index("reg")
    regions = lax.axis_size("reg")
    members, _, levels, rows, _ = pert_ref.shape
    height, pairs, _ = held_out.shape
    coarse_rows = height - 2
    ratio = rows // coarse_rows
    inner = levels * rows
    even = lax.rem(region, 2) == 0

    q = q_refs[0][...]
    for ref in q_refs[1:]:
        q = q + ref[...]
    q0, q1, q2, q3 = (q[n : n + 1] for n in range(4))
    kind = kind_ref[...]
    seen = jnp.where(kind == 0, q0, jnp.where(kind == 1, q1, jnp.where(kind == 2, q1 - q3, q0 * q2 + q1 * q3)))
    misfit = weight_ref[...] * (seen - value_ref[...])
    zero = jnp.zeros_like(misfit)
    a = jnp.where(kind == 0, misfit, jnp.where(kind == 3, misfit * q2, zero))
    b = jnp.where(kind == 2, -misfit, jnp.where(kind == 3, misfit * q1, zero))
    c = jnp.where(kind == 3, misfit * q0, zero)
    g = jnp.where(kind == 3, misfit * q3, jnp.where(kind == 0, zero, misfit))
    r0, ru, rv = r0_ref[...], ru_ref[...], rv_ref[...]
    lines = r0.shape[0]
    left = [r0 * x + ru * y for x, y in zip(split(a), split(c))] + [rv * x for x in split(g)]
    left = jnp.concatenate(left, axis=0)
    left_y = jnp.concatenate([r0[:inner] * x for x in split(b)], axis=0)
    both = dot_nt(left, c0_ref[...])
    along = dot_nt(left_y, cy_ref[...])
    total = both[:lines] + both[lines : 2 * lines]
    u_scr[pl.ds(0, inner), :] = total[:inner] + (along[:inner] + along[inner:])
    u_scr[pl.ds(inner, lines - inner), :] = total[inner:]
    v_scr[...] = both[2 * lines : 3 * lines] + both[3 * lines :]

    def project(products):
        high, lower = split(jnp.concatenate(products, axis=0))
        return dot_nn(high, down_ref[...]) + dot_nn(lower, down_ref[...])

    block = chunk * rows
    for s in range(levels // chunk):
        products = []
        for m in range(members):
            for k in range(s * chunk, (s + 1) * chunk):
                here = pl.ds(k * rows, rows)
                pu, pv = pert_ref[m, 0, k].astype(F32), pert_ref[m, 1, k].astype(F32)
                products.append(u_scr[here, :] * pu + v_scr[here, :] * pv)
        got = project(products)
        for m in range(members):
            f_scr[pl.ds(m * inner + s * block, block), :] = got[m * block : (m + 1) * block]

    edges = {}
    for n in range(2):
        rim = pl.ds(inner + n * levels, levels)
        u, v = u_scr[rim, :], v_scr[rim, :]
        found = []
        for m in range(members):
            halo = []
            for part in range(2):
                x, y = even_ref[m, part], odd_ref[m, part]
                halo.append(jnp.where(even, y, x) if n == 0 else jnp.where(even, x, y))
            found.append(u * halo[0] + v * halo[1])
        edges[-1 if n == 0 else rows] = project(found)

    held = {}
    for i in range(-1, rows + 1):
        value = edges[i] if i in edges else f_scr[pl.ds(i, pairs, stride=rows), :]
        low, w0, w1 = weights_x(i, ratio)
        for at, w in ((low, w0), (low + 1, w1)):
            held[at] = w * value if at not in held else held[at] + w * value
    held = {r: mask_row(value * scale, r, coarse_rows, region, regions) for r, value in held.items()}
    for r, value in held.items():
        held_out[r + 1] = value
    near = smooth_outside(held, even, twice_ref, once_ref)
    for k in range(HALO):
        b_out[k] = jnp.where(even, near[k - HALO], near[-1 - k])


def backward(q_terms, kind, value, weight, tables_y, pert, halo_even, halo_odd, hot, scale, coarse_rows, coarse_columns):
    members, _, levels, rows, columns = pert.shape
    pairs = members * levels
    outs = [jax.ShapeDtypeStruct((n, pairs, coarse_columns), F32) for n in (coarse_rows + 2, HALO)]
    return pl.pallas_call(
        functools.partial(backward_kernel, scale, 4 if levels % 4 == 0 else 1, len(q_terms)),
        out_shape=outs,
        scratch_shapes=[
            pltpu.VMEM((levels * rows + 2 * levels, columns), F32),
            pltpu.VMEM((levels * rows + 2 * levels, columns), F32),
            pltpu.VMEM((pairs * rows, coarse_columns), F32),
        ],
        compiler_params=params(28),
        name="adjoint_to_coarse",
    )(*q_terms, kind, value, weight, *tables_y, pert, halo_even, halo_odd, *hot)


def finish_kernel(held_ref, twice_ref, once_ref, own_out, a_out):
    region = lax.axis_index("reg")
    regions = lax.axis_size("reg")
    even = lax.rem(region, 2) == 0
    coarse_rows = own_out.shape[0]
    held = {r: held_ref[r + 1] for r in range(-1, coarse_rows + 1)}
    near = smooth_outside(held, jnp.logical_not(even), twice_ref, once_ref)
    for k in range(HALO):
        a_out[k] = jnp.where(even, near[-1 - k], near[k - HALO])
    own = smooth(held, range(coarse_rows), coarse_rows, region, regions, twice_ref[...], once_ref[...])
    for r in range(coarse_rows):
        own_out[r] = own[r]


def finish(held, tables_y):
    height, pairs, columns = held.shape
    return pl.pallas_call(
        finish_kernel,
        out_shape=[jax.ShapeDtypeStruct((n, pairs, columns), F32) for n in (height - 2, HALO)],
        compiler_params=params(16),
        name="finish_rows",
    )(held, *tables_y)


def join_kernel(coarse_rows, own_ref, even_ref, odd_ref, out_hbm, out_scr, sem):
    even = lax.rem(lax.axis_index("reg"), 2) == 0
    pairs = own_ref.shape[1]
    chunks = sem.shape[0]
    some = pairs // chunks
    copies = []
    for n in range(chunks):
        here = pl.ds(n * some, some)
        for r in range(coarse_rows):
            total = own_ref[r, here, :]
            if r < HALO:
                total = total + jnp.where(even, odd_ref[r, here, :], even_ref[r, here, :])
            k = r - (coarse_rows - HALO)
            if k >= 0:
                total = total + jnp.where(even, even_ref[k, here, :], odd_ref[k, here, :])
            out_scr[pl.ds(n * some * coarse_rows + r, some, stride=coarse_rows), :] = total
        block = pl.ds(n * some * coarse_rows, some * coarse_rows)
        copy = pltpu.make_async_copy(out_scr.at[block], out_hbm.at[block], sem.at[n])
        copy.start()
        copies.append(copy)
    for copy in copies:
        copy.wait()


def join(own, got_even, got_odd):
    coarse_rows, pairs, columns = own.shape
    chunks = 4 if pairs % 32 == 0 else 1
    vmem = pl.BlockSpec(memory_space=pltpu.VMEM)
    return pl.pallas_call(
        functools.partial(join_kernel, coarse_rows),
        in_specs=[vmem, vmem, vmem],
        out_specs=pl.BlockSpec(memory_space=pltpu.HBM),
        out_shape=jax.ShapeDtypeStruct((pairs * coarse_rows, columns), F32),
        scratch_shapes=[
            pltpu.VMEM((pairs * coarse_rows, columns), F32),
            pltpu.SemaphoreType.DMA((chunks,)),
        ],
        compiler_params=params(16),
        name="join_rows",
    )(own, got_even, got_odd)


def local(alpha, perturbation, obs_cell, obs_kind, obs_value, obs_weight):
    members, levels, coarse_rows, coarse_columns = alpha.shape
    _, _, _, rows, columns = perturbation.shape
    scale = 1.0 / math.sqrt(members * lax.axis_size("mem"))
    flat = alpha.reshape(-1, coarse_columns)
    cell, kind, value, weight = (x.reshape(1, -1) for x in (obs_cell, obs_kind, obs_value, obs_weight))
    down = down_weights(coarse_columns, columns)
    flat_odd = swap_odd(flat)
    flat_even = swap_even(flat)
    packed = pack(perturbation, 1)
    halo_odd = swap_odd(packed)
    packed = pack(perturbation, 0)
    halo_even = swap_even(packed)
    hot, along_y = tables(cell, kind, levels, rows, columns, coarse_columns)
    q, edge_fine = forward(flat, flat_even, flat_odd, along_y, perturbation, hot, scale)
    q = edge(q, edge_fine, halo_even, halo_odd, hot, members, levels)
    terms = others(q, "mem")
    held, send_b = backward(
        terms, kind, value, weight, (down, *along_y[1:]), perturbation, halo_even, halo_odd, hot, scale,
        coarse_rows, coarse_columns,
    )
    got_odd = swap_odd(send_b)
    own, send_a = finish(held, along_y[1:])
    got_even = swap_even(send_a)
    return join(own, got_even, got_odd).reshape(alpha.shape)


def solution(mesh):
    return jax.shard_map(
        local,
        mesh=mesh,
        in_specs=(
            P("mem", None, "reg", None),
            P("mem", None, None, "reg", None),
            P("reg"),
            P("reg"),
            P("reg"),
            P("reg"),
        ),
        out_specs=P("mem", None, "reg", None),
        check_vma=False,
    )
```

```python
import functools
import math

import jax
import jax.numpy as jnp
from jax import lax
from jax.experimental import pallas as pl
from jax.experimental.pallas import tpu as pltpu
from jax.sharding import PartitionSpec as P


PASSES = 2
HALO = PASSES + 1
DIFFUSE = 0.2
CENTRE = round((1.0 - 4.0 * DIFFUSE) / DIFFUSE)
F32 = jnp.float32
BF16 = jnp.bfloat16


def params(mib):
    return pltpu.CompilerParams(vmem_limit_bytes=mib << 20)


def swap_pairs(n, odd):
    pairs = []
    for i in range(1 if odd else 0, n - 1, 2):
        pairs += [(i, i + 1), (i + 1, i)]
    return pairs


def swap_even(value):
    return lax.ppermute(value, "reg", swap_pairs(lax.axis_size("reg"), False))


def swap_odd(value):
    return lax.ppermute(value, "reg", swap_pairs(lax.axis_size("reg"), True))


def others(value, axis):
    n = lax.axis_size(axis)
    stride = 1
    rounds = []
    while stride < n:
        left = n // stride
        radix = 4 if left % 4 == 0 else 2 if left % 2 == 0 else left
        sends = []
        for k in range(1, radix):
            pairs = []
            for i in range(n):
                digit = (i // stride) % radix
                other = digit ^ k if radix in (2, 4) else (digit + k) % radix
                pairs.append((i, i + (other - digit) * stride))
            sends.append(pairs)
        rounds.append(sends)
        stride *= radix
    for number, sends in enumerate(rounds):
        got = []
        for pairs in sends:
            got.append(lax.ppermute(value, axis, pairs))
        if number == len(rounds) - 1:
            return [value] + got
        for part in got:
            value = value + part
    return [value]


def split(x):
    high = x.astype(BF16)
    return high, (x - high.astype(F32)).astype(BF16)


def dot_nn(a, b):
    return lax.dot_general(a, b, (((1,), (0,)), ((), ())), preferred_element_type=F32)


def dot_nt(a, b):
    return lax.dot_general(a, b, (((1,), (1,)), ((), ())), preferred_element_type=F32)


def iota(shape, dim):
    return lax.broadcasted_iota(jnp.int32, shape, dim)


def table_y(coarse, fine, coarse_dim):
    shape = (coarse, fine) if coarse_dim == 0 else (fine, coarse)
    ratio = fine // coarse
    at = (iota(shape, 1 - coarse_dim).astype(F32) + 0.5) / ratio - 0.5
    return jnp.maximum(0.0, 1.0 - jnp.abs(at - iota(shape, coarse_dim).astype(F32))).astype(BF16)


def weights_x(i, ratio):
    at = (i + 0.5) / ratio - 0.5
    low = math.floor(at)
    return low, 1.0 - (at - low), at - low


def filters(columns):
    row, column = iota((columns, columns), 0), iota((columns, columns), 1)
    near = jnp.abs(row - column)
    once = jnp.where(near == 0, CENTRE, jnp.where(near == 1, 1.0, 0.0)).astype(BF16)
    twice = dot_nn(once, once).astype(BF16)
    once = once + once
    return jnp.concatenate([twice, twice], axis=0), jnp.concatenate([once, once], axis=0)


def smooth(rows, wanted, coarse_rows, region, regions, twice, once):
    pairs = next(iter(rows.values())).shape[0]

    def both(values):
        high, lower = split(jnp.concatenate(values, axis=0))
        return jnp.concatenate([high, lower], axis=1)

    def total(*names):
        found = [rows[n] for n in names if n in rows]
        return functools.reduce(jnp.add, found) if found else None

    mids = [r for r in wanted if r in rows]
    at_mid = dot_nn(both([rows[r] for r in mids]), twice)
    sides = [r for r in wanted if total(r - 1, r + 1) is not None]
    at_side = dot_nn(both([total(r - 1, r + 1) for r in sides]), once)
    out = {}
    for r in wanted:
        terms = []
        if r in mids:
            k = mids.index(r)
            terms.append(at_mid[k * pairs : (k + 1) * pairs])
            around = 2.0
            if r == 0:
                around = jnp.where(region > 0, 2.0, 1.0)
            elif r == coarse_rows - 1:
                around = jnp.where(region < regions - 1, 2.0, 1.0)
            terms.append(around * rows[r])
        if r in sides:
            k = sides.index(r)
            terms.append(at_side[k * pairs : (k + 1) * pairs])
        far = total(r - 2, r + 2)
        if far is not None:
            terms.append(far)
        out[r] = (DIFFUSE * DIFFUSE) * functools.reduce(jnp.add, terms)
    return out


def mask_row(value, index, coarse_rows, region, regions):
    if index < 0:
        return jnp.where(region * coarse_rows + index >= 0, value, 0.0)
    if index >= coarse_rows:
        return jnp.where(region * coarse_rows + index < regions * coarse_rows, value, 0.0)
    return value


def sides():
    odd = lax.rem(lax.axis_index("reg"), 2)
    return 1 - odd, odd


def decode(cell, rows, columns):
    plane = rows * columns
    level = cell // plane
    rest = cell - level * plane
    row = rest // columns
    return level, row, rest - row * columns


def down_kernel(down_ref):
    fine, coarse = down_ref.shape
    down_ref[...] = table_y(coarse, fine, 1)


def down_weights(coarse, fine):
    return pl.pallas_call(
        down_kernel,
        out_shape=jax.ShapeDtypeStruct((fine, coarse), BF16),
        compiler_params=params(16),
        cost_estimate=pl.CostEstimate(flops=1160000000, bytes_accessed=1 << 20, transcendentals=0),
        name="down_weights",
    )()


def pack_kernel(last_parity, pert_ref, out_ref):
    members, parts, levels, rows, columns = pert_ref.shape
    half = rows // 2
    last = jnp.where(lax.rem(lax.axis_index("reg"), 2) == last_parity, 1, 0)
    shape = (levels, levels * half)
    wanted = iota(shape, 0) * half + last * (half - 1)
    chooser = jnp.where(iota(shape, 1) == wanted, 1.0, 0.0).astype(BF16)
    inside = pl.ds(pl.multiple_of(last * half, half), half)
    for m in range(members):
        for part in range(parts):
            block = pert_ref[m, part, :, inside, :].reshape(levels * half, columns)
            out_ref[m, part] = dot_nn(chooser, block)


def pack(pert, last_parity):
    members, parts, levels, _, columns = pert.shape
    return pl.pallas_call(
        functools.partial(pack_kernel, last_parity),
        out_shape=jax.ShapeDtypeStruct((members, parts, levels, columns), F32),
        compiler_params=params(16),
    )(pert)


def tables_kernel(
    levels, rows, columns, cell_ref, kind_ref, r0_ref, ru_ref, rv_ref, c0_ref, cy_ref, up_ref, twice_ref, once_ref
):
    coarse = twice_ref.shape[1]
    up = table_y(coarse, columns, 0)
    up_ref[...] = jnp.concatenate([up, up], axis=0)
    twice_ref[...], once_ref[...] = filters(coarse)
    cell, kind = cell_ref[...], kind_ref[...]
    level, row, column = decode(cell, rows, columns)
    line = level * rows + row
    count = cell.shape[1]
    inner = levels * rows
    minus = jnp.where(row > 0, line - 1, inner + level)
    plus = jnp.where(row < rows - 1, line + 1, inner + levels + level)
    none = jnp.full_like(line, -1)
    minus_u = jnp.where(kind == 3, minus, none)
    plus_u = jnp.where(kind == 3, plus, none)
    here_v = jnp.where((kind == 1) | (kind == 3), line, none)
    minus_v = jnp.where(kind == 2, minus, none)
    plus_v = jnp.where(kind == 2, plus, none)
    step = 32

    def lines(k, _):
        start = pl.multiple_of(k * step, step)
        at = iota((step, count), 0) + start
        ru = jnp.where(at == plus_u, 0.5, jnp.where(at == minus_u, -0.5, 0.0))
        rv = jnp.where(at == plus_v, 0.5, jnp.where(at == minus_v, -0.5, jnp.where(at == here_v, 1.0, 0.0)))
        r0 = jnp.where(at == line, 1.0, 0.0)
        ru_ref[pl.ds(start, step), :] = ru.astype(BF16)
        rv_ref[pl.ds(start, step), :] = rv.astype(BF16)
        r0_ref[pl.ds(start, step), :] = r0.astype(BF16)
        return 0

    lax.fori_loop(0, (inner + 2 * levels) // step, lines, 0)

    def cells(k, _):
        start = pl.multiple_of(k * step, step)
        at = iota((step, count), 0) + start
        c0_ref[pl.ds(start, step), :] = jnp.where(at == column, 1.0, 0.0).astype(BF16)
        cy = jnp.where(at == column + 1, 0.5, jnp.where(at == column - 1, -0.5, 0.0))
        cy_ref[pl.ds(start, step), :] = cy.astype(BF16)
        return 0

    lax.fori_loop(0, columns // step, cells, 0)


def tables(cell, kind, levels, rows, columns, coarse):
    count = cell.shape[1]
    lines = levels * rows + 2 * levels
    shapes = [(n, count) for n in (lines, lines, lines, columns, columns)]
    shapes += [(2 * coarse, columns), (2 * coarse, coarse), (2 * coarse, coarse)]
    made = pl.pallas_call(
        functools.partial(tables_kernel, levels, rows, columns),
        out_shape=[jax.ShapeDtypeStruct(shape, BF16) for shape in shapes],
        compiler_params=params(16),
        name="one_hots",
    )(cell, kind)
    return made[:5], made[5:]


def forward_kernel(
    scale, chunk,
    own_ref, even_ref, odd_ref, up_ref, twice_ref, once_ref, pert_ref, r0_ref, ru_ref, rv_ref, c0_ref, cy_ref,
    q_ref, edge_ref,
    fine_in, fine_scr, t_scr,
):
    region = lax.axis_index("reg")
    regions = lax.axis_size("reg")
    members, _, levels, rows, _ = pert_ref.shape
    pairs = members * levels
    coarse_rows = own_ref.shape[0] // pairs
    ratio = rows // coarse_rows
    block = chunk * rows
    inner = levels * rows
    even = lax.rem(region, 2) == 0
    table = up_ref[...]
    rows_in = {r: own_ref[pl.ds(r, pairs, stride=coarse_rows), :] for r in range(coarse_rows)}
    for k in range(HALO):
        low = coarse_rows - HALO + k
        e = even_ref[pl.ds(low, pairs, stride=coarse_rows), :]
        o = odd_ref[pl.ds(low, pairs, stride=coarse_rows), :]
        rows_in[k - HALO] = jnp.where(even, o, e)
        e = even_ref[pl.ds(k, pairs, stride=coarse_rows), :]
        o = odd_ref[pl.ds(k, pairs, stride=coarse_rows), :]
        rows_in[coarse_rows + k] = jnp.where(even, e, o)
    rows_in = smooth(
        rows_in, range(-1, coarse_rows + 1), coarse_rows, region, regions, twice_ref[...], once_ref[...]
    )
    rows_in = {r: mask_row(value, r, coarse_rows, region, regions) for r, value in rows_in.items()}
    for i in range(-1, rows + 1):
        low, w0, w1 = weights_x(i, ratio)
        value = (w0 * rows_in[low] + w1 * rows_in[low + 1]) * scale
        if 0 <= i < rows:
            fine_in[pl.ds(i, pairs, stride=rows), :] = value
        else:
            high, lower = split(value)
            got = dot_nn(jnp.concatenate([high, lower], axis=1), table)
            edge_ref[0 if i < 0 else 1] = got

    for step in range(levels // chunk):
        parts = []
        for m in range(members):
            parts.append(fine_in[pl.ds(m * inner + step * block, block), :])
        high, lower = split(jnp.concatenate(parts, axis=0))
        fine_scr[step % 2] = dot_nn(jnp.concatenate([high, lower], axis=1), table)
        for k in range(chunk):
            u = v = None
            for m in range(members):
                fine = fine_scr[step % 2, pl.ds(m * block + k * rows, rows), :]
                pu = fine * pert_ref[m, 0, step * chunk + k].astype(F32)
                pv = fine * pert_ref[m, 1, step * chunk + k].astype(F32)
                u = pu if u is None else u + pu
                v = pv if v is None else v + pv
            for n, value in enumerate((*split(u), *split(v))):
                t_scr[pl.ds(n * inner + step * block + k * rows, rows), :] = value

    count = r0_ref.shape[1]
    width = min(256, count)
    for k in range(count // width):
        at = pl.ds(k * width, width)
        z = dot_nn(t_scr[...], c0_ref[:, at])
        zy = dot_nn(t_scr[pl.ds(0, 2 * inner), :], cy_ref[:, at])
        zu = z[:inner] + z[inner : 2 * inner]
        zv = z[2 * inner : 3 * inner] + z[3 * inner :]
        zy = zy[:inner] + zy[inner:]
        inside = pl.ds(0, inner)
        r0 = r0_ref[inside, at].astype(F32)
        q_ref[pl.ds(0, 1), at] = jnp.sum(r0 * zu, axis=0, keepdims=True)
        q_ref[pl.ds(1, 1), at] = jnp.sum(rv_ref[inside, at].astype(F32) * zv, axis=0, keepdims=True)
        q_ref[pl.ds(2, 1), at] = jnp.sum(ru_ref[inside, at].astype(F32) * zu, axis=0, keepdims=True)
        q_ref[pl.ds(3, 1), at] = jnp.sum(r0 * zy, axis=0, keepdims=True)


def forward(own, got_even, got_odd, weight, pert, hot, scale):
    up, twice, once = weight
    members, _, levels, rows, columns = pert.shape
    pairs, coarse_columns = members * levels, own.shape[1]
    chunk = 4 if levels % 4 == 0 else 1
    count = hot[0].shape[1]
    return pl.pallas_call(
        functools.partial(forward_kernel, scale, chunk),
        out_shape=[jax.ShapeDtypeStruct((4, count), F32),
                   jax.ShapeDtypeStruct((2, pairs, columns), F32)],
        scratch_shapes=[
            pltpu.VMEM((pairs * rows, coarse_columns), F32),
            pltpu.VMEM((2, members * chunk * rows, columns), F32),
            pltpu.VMEM((4 * levels * rows, columns), BF16),
        ],
        compiler_params=params(28),
        name="increment_at_obs",
    )(own, got_even, got_odd, up, twice, once, pert, *hot)


def edge_kernel(odd, members, levels, q_ref, fine_ref, halo_ref, ru_ref, rv_ref, c0_ref, out_ref):
    near = sides()[odd]
    lines = ru_ref.shape[0]
    inner = lines - 2 * levels
    table = []
    for part in range(2):
        total = None
        for m in range(members):
            term = fine_ref[near, pl.ds(m * levels, levels), :] * halo_ref[m, part]
            total = term if total is None else total + term
        table.append(total)
    high, lower = split(jnp.concatenate(table, axis=0))
    z = dot_nn(jnp.concatenate([high, lower], axis=0), c0_ref[...])
    z = z[: 2 * levels] + z[2 * levels :]
    here = pl.ds(pl.multiple_of(inner + near * levels, levels), levels)
    in_u = jnp.sum(ru_ref[here, :].astype(F32) * z[:levels], axis=0, keepdims=True)
    in_v = jnp.sum(rv_ref[here, :].astype(F32) * z[levels:], axis=0, keepdims=True)
    out_ref[pl.ds(0, 1), :] = q_ref[pl.ds(0, 1), :]
    out_ref[pl.ds(1, 1), :] = q_ref[pl.ds(1, 1), :] + in_v
    out_ref[pl.ds(2, 1), :] = q_ref[pl.ds(2, 1), :] + in_u
    out_ref[pl.ds(3, 1), :] = q_ref[pl.ds(3, 1), :]


def edge(q, fine, halo, odd, hot, members, levels):
    _, ru, rv, c0, _ = hot
    return pl.pallas_call(
        functools.partial(edge_kernel, odd, members, levels),
        out_shape=jax.ShapeDtypeStruct(q.shape, F32),
        compiler_params=pltpu.CompilerParams(vmem_limit_bytes=16 << 20),
    )(q, fine, halo, ru, rv, c0)


def smooth_outside(held, before, twice_ref, once_ref):
    last = max(held) - 1
    rows = {r: jnp.where(before, held[r], held[last - r]) for r in range(-1, PASSES)}
    return smooth(rows, range(-HALO, 0), last + 1, 0, 1, twice_ref[...], once_ref[...])


def backward_kernel(scale, chunk, terms, *refs):
    q_refs = refs[:terms]
    (kind_ref, value_ref, weight_ref, down_ref, twice_ref, once_ref, pert_ref, even_ref, odd_ref,
     r0_ref, ru_ref, rv_ref, c0_ref, cy_ref,
     held_out, b_out,
     u_scr, v_scr, f_scr) = refs[terms:]
    region = lax.axis_index("reg")
    regions = lax.axis_size("reg")
    members, _, levels, rows, _ = pert_ref.shape
    height, pairs, _ = held_out.shape
    coarse_rows = height - 2
    ratio = rows // coarse_rows
    inner = levels * rows
    even = lax.rem(region, 2) == 0

    q = q_refs[0][...]
    for ref in q_refs[1:]:
        q = q + ref[...]
    q0, q1, q2, q3 = (q[n : n + 1] for n in range(4))
    kind = kind_ref[...]
    seen = jnp.where(kind == 0, q0, jnp.where(kind == 1, q1, jnp.where(kind == 2, q1 - q3, q0 * q2 + q1 * q3)))
    misfit = weight_ref[...] * (seen - value_ref[...])
    zero = jnp.zeros_like(misfit)
    a = jnp.where(kind == 0, misfit, jnp.where(kind == 3, misfit * q2, zero))
    b = jnp.where(kind == 2, -misfit, jnp.where(kind == 3, misfit * q1, zero))
    c = jnp.where(kind == 3, misfit * q0, zero)
    g = jnp.where(kind == 3, misfit * q3, jnp.where(kind == 0, zero, misfit))
    r0, ru, rv = r0_ref[...], ru_ref[...], rv_ref[...]
    lines = r0.shape[0]
    left = [r0 * x + ru * y for x, y in zip(split(a), split(c))] + [rv * x for x in split(g)]
    left = jnp.concatenate(left, axis=0)
    left_y = jnp.concatenate([r0[:inner] * x for x in split(b)], axis=0)
    both = dot_nt(left, c0_ref[...])
    along = dot_nt(left_y, cy_ref[...])
    total = both[:lines] + both[lines : 2 * lines]
    u_scr[pl.ds(0, inner), :] = total[:inner] + (along[:inner] + along[inner:])
    u_scr[pl.ds(inner, lines - inner), :] = total[inner:]
    v_scr[...] = both[2 * lines : 3 * lines] + both[3 * lines :]

    def project(products):
        high, lower = split(jnp.concatenate(products, axis=0))
        return dot_nn(high, down_ref[...]) + dot_nn(lower, down_ref[...])

    block = chunk * rows
    for s in range(levels // chunk):
        products = []
        for m in range(members):
            for k in range(s * chunk, (s + 1) * chunk):
                here = pl.ds(k * rows, rows)
                pu, pv = pert_ref[m, 0, k].astype(F32), pert_ref[m, 1, k].astype(F32)
                products.append(u_scr[here, :] * pu + v_scr[here, :] * pv)
        got = project(products)
        for m in range(members):
            f_scr[pl.ds(m * inner + s * block, block), :] = got[m * block : (m + 1) * block]

    edges = {}
    for n in range(2):
        rim = pl.ds(inner + n * levels, levels)
        u, v = u_scr[rim, :], v_scr[rim, :]
        found = []
        for m in range(members):
            halo = []
            for part in range(2):
                x, y = even_ref[m, part], odd_ref[m, part]
                halo.append(jnp.where(even, y, x) if n == 0 else jnp.where(even, x, y))
            found.append(u * halo[0] + v * halo[1])
        edges[-1 if n == 0 else rows] = project(found)

    held = {}
    for i in range(-1, rows + 1):
        value = edges[i] if i in edges else f_scr[pl.ds(i, pairs, stride=rows), :]
        low, w0, w1 = weights_x(i, ratio)
        for at, w in ((low, w0), (low + 1, w1)):
            held[at] = w * value if at not in held else held[at] + w * value
    held = {r: mask_row(value * scale, r, coarse_rows, region, regions) for r, value in held.items()}
    for r, value in held.items():
        held_out[r + 1] = value
    near = smooth_outside(held, even, twice_ref, once_ref)
    for k in range(HALO):
        b_out[k] = jnp.where(even, near[k - HALO], near[-1 - k])


def backward(q_terms, kind, value, weight, tables_y, pert, halo_even, halo_odd, hot, scale, coarse_rows, coarse_columns):
    members, _, levels, rows, columns = pert.shape
    pairs = members * levels
    outs = [jax.ShapeDtypeStruct((n, pairs, coarse_columns), F32) for n in (coarse_rows + 2, HALO)]
    return pl.pallas_call(
        functools.partial(backward_kernel, scale, 4 if levels % 4 == 0 else 1, len(q_terms)),
        out_shape=outs,
        scratch_shapes=[
            pltpu.VMEM((levels * rows + 2 * levels, columns), F32),
            pltpu.VMEM((levels * rows + 2 * levels, columns), F32),
            pltpu.VMEM((pairs * rows, coarse_columns), F32),
        ],
        compiler_params=pltpu.CompilerParams(vmem_limit_bytes=28 << 20),
        name="adjoint_to_coarse",
    )(*q_terms, kind, value, weight, *tables_y, pert, halo_even, halo_odd, *hot)


def finish_kernel(held_ref, twice_ref, once_ref, own_out, a_out):
    region = lax.axis_index("reg")
    regions = lax.axis_size("reg")
    even = lax.rem(region, 2) == 0
    coarse_rows = own_out.shape[0]
    held = {r: held_ref[r + 1] for r in range(-1, coarse_rows + 1)}
    near = smooth_outside(held, jnp.logical_not(even), twice_ref, once_ref)
    for k in range(HALO):
        a_out[k] = jnp.where(even, near[-1 - k], near[k - HALO])
    own = smooth(held, range(coarse_rows), coarse_rows, region, regions, twice_ref[...], once_ref[...])
    for r in range(coarse_rows):
        own_out[r] = own[r]


def finish(held, tables_y):
    height, pairs, columns = held.shape
    return pl.pallas_call(
        finish_kernel,
        out_shape=[jax.ShapeDtypeStruct((n, pairs, columns), F32) for n in (height - 2, HALO)],
        compiler_params=params(16),
        name="finish_rows",
    )(held, *tables_y)


def join_kernel(coarse_rows, own_ref, even_ref, odd_ref, out_hbm, out_scr, sem):
    even = lax.rem(lax.axis_index("reg"), 2) == 0
    pairs = own_ref.shape[1]
    chunks = sem.shape[0]
    some = pairs // chunks
    copies = []
    for n in range(chunks):
        here = pl.ds(n * some, some)
        for r in range(coarse_rows):
            total = own_ref[r, here, :]
            if r < HALO:
                total = total + jnp.where(even, odd_ref[r, here, :], even_ref[r, here, :])
            k = r - (coarse_rows - HALO)
            if k >= 0:
                total = total + jnp.where(even, even_ref[k, here, :], odd_ref[k, here, :])
            out_scr[pl.ds(n * some * coarse_rows + r, some, stride=coarse_rows), :] = total
        block = pl.ds(n * some * coarse_rows, some * coarse_rows)
        copy = pltpu.make_async_copy(out_scr.at[block], out_hbm.at[block], sem.at[n])
        copy.start()
        copies.append(copy)
    for copy in copies:
        copy.wait()


def join(own, got_even, got_odd):
    coarse_rows, pairs, columns = own.shape
    chunks = 4 if pairs % 32 == 0 else 1
    vmem = pl.BlockSpec(memory_space=pltpu.VMEM)
    return pl.pallas_call(
        functools.partial(join_kernel, coarse_rows),
        in_specs=[vmem, vmem, vmem],
        out_specs=pl.BlockSpec(memory_space=pltpu.HBM),
        out_shape=jax.ShapeDtypeStruct((pairs * coarse_rows, columns), F32),
        scratch_shapes=[
            pltpu.VMEM((pairs * coarse_rows, columns), F32),
            pltpu.SemaphoreType.DMA((chunks,)),
        ],
        compiler_params=params(16),
        name="join_rows",
    )(own, got_even, got_odd)


def local(alpha, perturbation, obs_cell, obs_kind, obs_value, obs_weight):
    members, levels, coarse_rows, coarse_columns = alpha.shape
    _, _, _, rows, columns = perturbation.shape
    scale = 1.0 / math.sqrt(members * lax.axis_size("mem"))
    flat = alpha.reshape(-1, coarse_columns)
    cell, kind, value, weight = (x.reshape(1, -1) for x in (obs_cell, obs_kind, obs_value, obs_weight))
    down = down_weights(coarse_columns, columns)
    flat_odd = swap_odd(flat)
    flat_even = swap_even(flat)
    packed = pack(perturbation, 1)
    halo_odd = swap_odd(packed)
    packed = pack(perturbation, 0)
    halo_even = swap_even(packed)
    hot, along_y = tables(cell, kind, levels, rows, columns, coarse_columns)
    q, edge_fine = forward(flat, flat_even, flat_odd, along_y, perturbation, hot, scale)
    q = edge(q, edge_fine, halo_even, 0, hot, members, levels)
    q = edge(q, edge_fine, halo_odd, 1, hot, members, levels)
    terms = others(q, "mem")
    held, send_b = backward(
        terms, kind, value, weight, (down, *along_y[1:]), perturbation, halo_even, halo_odd, hot, scale,
        coarse_rows, coarse_columns,
    )
    got_odd = swap_odd(send_b)
    own, send_a = finish(held, along_y[1:])
    got_even = swap_even(send_a)
    return join(own, got_even, got_odd).reshape(alpha.shape)


def solution(mesh):
    return jax.shard_map(
        local,
        mesh=mesh,
        in_specs=(
            P("mem", None, "reg", None),
            P("mem", None, None, "reg", None),
            P("reg"),
            P("reg"),
            P("reg"),
            P("reg"),
        ),
        out_specs=P("mem", None, "reg", None),
        check_vma=False,
    )
```
